256 devices in a mesh: ctx: 32 (over y, x, core), head: 8 (over z).
Axes of the slice: x: 4, y: 4, z: 8, core: 2. Of those that a mesh axis runs over, the one named last changes fastest.
Arguments:
- hidden_in: bfloat16 [8192, 2048], P('ctx'), may hold values from -6 to 6
- gain_attn: float32 [2048], replicated, may hold values from 0.1 to 1.9
- w_qkv: bfloat16 [2048, 3, 2048], P(None, None, 'head'), may hold values from -0.125 to 0.125
- conv_w: float32 [4, 3, 2048], P(None, None, 'head'), may hold values from -3 to 3
- log_decay: float32 [8192, 16], P('ctx', 'head'), may hold values from -1 to 0, as said below
- norm_gain: float32 [2048], P('head'), may hold values from 0.1 to 1.9
- w_out: bfloat16 [2048, 2048], P('head'), may hold values from -0.125 to 0.125
- gain_moe: float32 [2048], replicated, may hold values from 0.1 to 1.9
- expert_ids: int32 [8192, 8], P('ctx'), may hold values from 0 to 63, all different within a row; in each aligned block of 256 rows (0 to 255, 256 to 511, ...) at most 48 rows name the same one
- route_weights: float32 [8192, 8], P('ctx'), may hold values from 0.05 to 1
- w_gate: bfloat16 [256, 2048, 256], P(('ctx', 'head')), may hold values from -0.125 to 0.125
- w_up: bfloat16 [256, 2048, 256], P(('ctx', 'head')), may hold values from -0.125 to 0.125
- w_down: bfloat16 [256, 256, 2048], P(('ctx', 'head')), may hold values from -0.1875 to 0.1875
- grad_core: bfloat16 [8192, 2048], P('ctx', 'head'), may hold values from -6 to 6
Outputs:
- layer_out: bfloat16 [8192, 2048], P('ctx', 'head')
- grad_q: bfloat16 [8192, 2048], P('ctx', 'head')
- grad_k: bfloat16 [8192, 2048], P('ctx', 'head')
- grad_v: bfloat16 [8192, 2048], P('ctx', 'head')
The draws below stay inside these ranges and needn't reach their ends.
Inputs may be any that keep to these rules, and one draw needn't show every extreme that they name: `expert_ids`: in each aligned block of 256 rows (the tokens of one index of ctx) no expert is chosen by more than 48 rows, a bound that some block reaches; the 8 experts of a row differ. `log_decay`: every entry is negative.
All inputs are finite; a program needn't handle non-finite values.
Results may differ from the reference program's by a relative error of at most 0.023.
Values may be sent and summed in bfloat16 or wider, within the bound.
A program may use at most 128 MiB of HBM per device.

```python
import math
import jax
import jax.numpy as jnp
import numpy as np
from jax import lax

D = 2048
ATTENDER_NUMBER = 16
DH = 128
HD = 2048
KERNEL = 4
FFE = 1024
TOP = 8
TOK_DEV = 256
SEGMENT_WORDS = 8192
EXPERTS = 64
SHARDS = 4
FF_DEV = 256
CAP = 48
N_CTX = 32


def draw_log_decay(key, part):
    lookup_array = jax.random.split(jax.random.fold_in(key, 7), 6)
    share = 0.5
    quick = jax.random.uniform(lookup_array[0], (ATTENDER_NUMBER,)) < share
    fast = jnp.exp(jax.random.uniform(lookup_array[1], (ATTENDER_NUMBER,), minval=math.log(1.0 / 50.0), maxval=math.log(1.0 / 30.0)))
    slow = jnp.exp(jax.random.uniform(lookup_array[2], (ATTENDER_NUMBER,), minval=math.log(0.1), maxval=math.log(0.5))) / SEGMENT_WORDS
    forgetting_speed = jnp.where(quick, fast, slow)
    multiplier_coefficient = jnp.exp(jax.random.uniform(lookup_array[3], (SEGMENT_WORDS, ATTENDER_NUMBER), minval=math.log(0.5), maxval=math.log(2.0)))
    spurt_extent = jax.random.uniform(lookup_array[4], (SEGMENT_WORDS, ATTENDER_NUMBER)) < 2.0 / SEGMENT_WORDS
    discarded_words = jnp.log(jax.random.uniform(lookup_array[5], (SEGMENT_WORDS, ATTENDER_NUMBER), minval=0.5, maxval=0.8))
    return (-forgetting_speed[None, :] * multiplier_coefficient + jnp.where(spurt_extent, discarded_words, 0.0)).astype(jnp.float32)


def shard_levels(own_key, extent, cuts, least, top_value):
    level, own = 1.0, jax.random.fold_in(own_key, 6)
    for axis_at, blocks in cuts:
        steps = jnp.exp(jax.random.uniform(jax.random.fold_in(own, axis_at), (blocks,), jnp.float32, least / len(cuts), top_value / len(cuts)))
        level = level * jnp.repeat(steps, extent[axis_at] // blocks).reshape([-1 if axis == axis_at else 1 for axis in range(len(extent))])
    return level


def shared_out(stream_key, own, number, rows, amount, top, bound, skew):
    ranking = jax.random.permutation(stream_key, amount)
    packed, ordinary = load_shares(amount, rows * top, bound, skew, True), load_shares(amount, rows * top, bound, skew, False)
    places = jnp.arange(amount)

    def named(sizes, rotation):
        used = int((sizes > 0).sum())
        fixed = max(1, used // 4)
        shifted = fixed + (places - fixed + rotation * (used - fixed)) % max(1, amount - fixed)
        return jnp.zeros((amount,), jnp.int32).at[ranking[jnp.where(places < fixed, places, shifted)]].set(jnp.asarray(sizes, jnp.int32))

    sizes = jnp.where(number % 4 == 0, named(packed, number // 4), named(ordinary, number - number // 4 - 1))
    mixed = jax.random.permutation(jax.random.fold_in(own, 3), amount)
    giver, taker = mixed[0:amount // 2 * 2:2], mixed[1:amount // 2 * 2:2]
    slack = jnp.minimum(sizes[giver] - 1, bound - sizes[taker]) // 2
    slack = jnp.where((giver == ranking[0]) | (taker == ranking[0]) | (sizes[taker] == 0), 0, jnp.maximum(slack, 0))
    shifted = jax.random.randint(jax.random.fold_in(own, 4), (amount // 2,), 0, 1 << 20) % (slack + 1)
    sizes = sizes.at[giver].add(-shifted).at[taker].add(shifted)
    items = jnp.searchsorted(jnp.cumsum(sizes), jnp.arange(rows * top), side="right").astype(jnp.int32)
    table = items.reshape(top, rows).T
    table = table[jax.random.permutation(jax.random.fold_in(own, 1), rows)]
    rotation = jax.random.randint(jax.random.fold_in(own, 2), (rows, 1), 0, top)
    return jnp.take_along_axis(table, (jnp.arange(top)[None, :] + rotation) % top, axis=1)


def load_shares(amount, total, bound, lean, full):
    portions = [(1 << 20) // math.isqrt(standing ** lean) + 1 for standing in range(1, amount + 1)]
    largest = bound if full else min(bound, max(-(-total // amount), total * portions[0] // sum(portions)))
    least = 1 if total - largest >= amount - 1 else 0
    given, spare = [largest] + [least] * (amount - 1), total - largest - least * (amount - 1)
    while spare > 0:
        movable = [i for i in range(1, amount) if given[i] < largest] or [i for i in range(1, amount) if given[i] < bound]
        pool, budget = sum([portions[i] for i in movable]), spare
        for i in movable:
            extra = min(bound - given[i], max(1, budget * portions[i] // pool), spare)
            given[i] = given[i] + extra
            spare = spare - extra
    return np.array(given)


def centred(own_key, extent, width, reach, cuts=(), kind=jnp.bfloat16):
    values = width * jax.random.normal(own_key, extent, jnp.float32)
    if cuts:
        values = values * shard_levels(own_key, extent, cuts, -0.22, 0.18)
    return jnp.clip(values, -reach, reach).astype(kind)


def setup_inputs(seed: int = 0) -> dict:
    splits = jax.random.split(jax.random.key(seed), 15)
    hidden_in = centred(splits[0], (SEGMENT_WORDS, D), 1.0, 6.0, ((0, 32),))
    gain_attn = jnp.clip(1.0 + 0.18 * jax.random.normal(splits[1], (D,), jnp.float32), 0.1, 1.9)
    w_qkv = centred(splits[2], (D, 3, HD), D ** -0.5, 0.125, ((2, 8),))
    conv_w = centred(splits[3], (KERNEL, 3, HD), KERNEL ** -0.5, 3.0, ((2, 8),), jnp.float32)
    log_decay = draw_log_decay(jax.random.fold_in(splits[14], 71), 0)
    norm_gain = jnp.clip(1.0 + 0.18 * jax.random.normal(splits[5], (HD,), jnp.float32), 0.1, 1.9)
    w_out = centred(splits[6], (HD, D), HD ** -0.5, 0.125, ((0, 8),))
    gain_moe = jnp.clip(1.0 + 0.18 * jax.random.normal(splits[7], (D,), jnp.float32), 0.1, 1.9)
    expert_ids_keys = jax.random.split(jax.random.fold_in(splits[8], 1), SEGMENT_WORDS // TOK_DEV)
    expert_ids_turns = jax.random.permutation(jax.random.fold_in(splits[8], 3), SEGMENT_WORDS // TOK_DEV)
    expert_ids = jax.vmap(lambda own, number: shared_out(jax.random.fold_in(splits[8], 2), own, number, TOK_DEV, EXPERTS, TOP, CAP, 2))(expert_ids_keys, expert_ids_turns).reshape((SEGMENT_WORDS, TOP))
    route_weights = jnp.clip(jnp.exp(math.log(1.0) - 2.9957323 * jax.random.uniform(splits[9], (SEGMENT_WORDS, TOP), jnp.float32) ** shard_levels(splits[9], (SEGMENT_WORDS, TOP), ((0, 32),), -0.2, 0.2)), 0.05, 1.0)
    w_gate = centred(splits[10], (EXPERTS * SHARDS, D, FF_DEV), D ** -0.5, 0.125, ((0, 256),))
    w_up = centred(splits[11], (EXPERTS * SHARDS, D, FF_DEV), D ** -0.5, 0.125, ((0, 256),))
    w_down = centred(splits[12], (EXPERTS * SHARDS, FF_DEV, D), FFE ** -0.5, 0.1875, ((0, 256),))
    grad_core = centred(splits[13], (SEGMENT_WORDS, HD), 1.0, 6.0, ((0, 32), (1, 8)))
    return {"hidden_in": hidden_in, "gain_attn": gain_attn, "w_qkv": w_qkv, "conv_w": conv_w, "log_decay": log_decay, "norm_gain": norm_gain, "w_out": w_out, "gain_moe": gain_moe, "expert_ids": expert_ids, "route_weights": route_weights, "w_gate": w_gate, "w_up": w_up, "w_down": w_down, "grad_core": grad_core}


def rms_norm(values, gain):
    return values * lax.rsqrt(lax.optimization_barrier(jnp.mean(values * values, axis=-1, keepdims=True)) + 1e-06) * gain

def short_conv(mixed, conv_w):
    lead = jnp.zeros((KERNEL - 1,) + mixed.shape[1:], jnp.float32)
    padded = jnp.concatenate([lead, mixed.astype(jnp.float32)], axis=0)
    total = jnp.zeros(mixed.shape, jnp.float32)
    for offset in range(KERNEL):
        total = total + conv_w[offset] * padded[KERNEL - 1 - offset:KERNEL - 1 - offset + mixed.shape[0]]
    return total

def linear_core(query_f, key_f, value_f, log_steps):
    blocks = SEGMENT_WORDS // TOK_DEV
    hi = lax.Precision.HIGHEST

    def block_step(state, items):
        q_blk, k_blk, v_blk, g_blk = items
        cum = jnp.cumsum(g_blk, axis=0)
        cum_t = cum.T
        diff = cum_t[:, :, None] - cum_t[:, None, :]
        lower = (jnp.arange(TOK_DEV)[:, None] >= jnp.arange(TOK_DEV)[None, :])[None]
        weights = jnp.where(lower, jnp.exp(jnp.where(lower, diff, 0.0)), 0.0)
        scores = jnp.einsum('thd,shd->hts', q_blk, k_blk, precision=hi) * weights
        local = jnp.einsum('hts,shd->thd', scores, v_blk, precision=hi)
        carried = jnp.einsum('thd,hde->the', q_blk, state, precision=hi) * jnp.exp(cum)[:, :, None]
        tail = jnp.exp(cum[-1][None, :] - cum)
        fresh = jnp.einsum('shd,she->hde', k_blk * tail[:, :, None], v_blk, precision=hi)
        new_state = jnp.exp(cum[-1])[:, None, None] * state + fresh
        return (new_state, local + carried)
    shaped = (blocks, TOK_DEV, ATTENDER_NUMBER, DH)
    items = (query_f.reshape(shaped), key_f.reshape(shaped), value_f.reshape(shaped), log_steps.reshape(blocks, TOK_DEV, ATTENDER_NUMBER))
    _, outs = lax.scan(block_step, jnp.zeros((ATTENDER_NUMBER, DH, DH), jnp.float32), items)
    return outs.reshape(SEGMENT_WORDS, ATTENDER_NUMBER, DH)

def mixture(moe_in, expert_ids, route_weights, w_gate, w_up, w_down):
    hi = lax.Precision.HIGHEST
    ids = expert_ids.reshape(N_CTX, TOK_DEV, TOP)
    hot = (ids[..., None] == jnp.arange(EXPERTS, dtype=jnp.int32)).astype(jnp.int32)
    counts = lax.optimization_barrier(jnp.sum(hot, axis=2))
    ranks = jnp.cumsum(counts, axis=1) - counts
    slot = lax.optimization_barrier(jnp.sum(hot * ranks[:, :, None, :], axis=-1))
    source = jnp.broadcast_to(jnp.arange(N_CTX, dtype=jnp.int32)[:, None, None], ids.shape)
    token = source * TOK_DEV + jnp.broadcast_to(jnp.arange(TOK_DEV, dtype=jnp.int32)[None, :, None], ids.shape)
    position = source * CAP + slot
    tok_table = jnp.full((EXPERTS, N_CTX * CAP), SEGMENT_WORDS, jnp.int32)
    tok_table = tok_table.at[ids.reshape(-1), position.reshape(-1)].set(token.reshape(-1))
    wt_table = jnp.zeros((EXPERTS, N_CTX * CAP), jnp.float32)
    wt_table = wt_table.at[ids.reshape(-1), position.reshape(-1)].set(route_weights.reshape(-1))
    padded_rows = jnp.concatenate([moe_in, jnp.zeros((1, D), jnp.bfloat16)], axis=0)
    gates = w_gate.reshape(EXPERTS, SHARDS, D, FF_DEV)
    ups = w_up.reshape(EXPERTS, SHARDS, D, FF_DEV)
    downs = w_down.reshape(EXPERTS, SHARDS, FF_DEV, D)

    def expert_step(total, items):
        row_index, row_weight, gate_e, up_e, down_e = items
        rows = padded_rows[row_index].astype(jnp.float32)
        summed = jnp.zeros((N_CTX * CAP, D), jnp.float32)
        for shard in range(SHARDS):
            gate_val = jnp.dot(rows, gate_e[shard].astype(jnp.float32), precision=hi)
            up_val = jnp.dot(rows, up_e[shard].astype(jnp.float32), precision=hi)
            inner = (jax.nn.silu(gate_val) * up_val).astype(jnp.bfloat16)
            part = jnp.dot(inner.astype(jnp.float32), down_e[shard].astype(jnp.float32), precision=hi)
            part = lax.optimization_barrier(part.astype(jnp.bfloat16))
            summed = summed + part.astype(jnp.float32)
        total = total.at[row_index].add(row_weight[:, None] * summed)
        return (total, None)
    start = jnp.zeros((SEGMENT_WORDS + 1, D), jnp.float32)
    total, _ = lax.scan(expert_step, start, (tok_table, wt_table, gates, ups, downs))
    return total[:SEGMENT_WORDS]

def reference(hidden_in, gain_attn, w_qkv, conv_w, log_decay, norm_gain, w_out, gain_moe, expert_ids, route_weights, w_gate, w_up, w_down, grad_core):
    x_float = hidden_in.astype(jnp.float32)
    normed = rms_norm(x_float, gain_attn).astype(jnp.bfloat16)
    mixed = jnp.dot(normed, w_qkv.reshape(D, 3 * HD), preferred_element_type=jnp.float32)
    mixed = mixed.astype(jnp.bfloat16).reshape(SEGMENT_WORDS, 3, HD)
    activ = jax.nn.silu(short_conv(mixed, conv_w))
    shape3 = (SEGMENT_WORDS, ATTENDER_NUMBER, DH)
    queries = (activ[:, 0] * DH ** (-0.5)).astype(jnp.bfloat16).astype(jnp.float32).reshape(shape3)
    key_rows = activ[:, 1].astype(jnp.bfloat16).astype(jnp.float32).reshape(shape3)
    val_rows = activ[:, 2].astype(jnp.bfloat16).astype(jnp.float32).reshape(shape3)

    def core_of(query_f, key_f, value_f):
        return linear_core(query_f, key_f, value_f, log_decay)
    attended, pullback = jax.vjp(core_of, queries, key_rows, val_rows)
    grad_q, grad_k, grad_v = pullback(grad_core.astype(jnp.float32).reshape(shape3))
    headed = rms_norm(attended, norm_gain.reshape(ATTENDER_NUMBER, DH)).reshape(SEGMENT_WORDS, HD).astype(jnp.bfloat16)
    resid = x_float + jnp.dot(headed, w_out, preferred_element_type=jnp.float32)
    moe_in = rms_norm(resid, gain_moe).astype(jnp.bfloat16)
    moe_out = mixture(moe_in, expert_ids, route_weights, w_gate, w_up, w_down)
    layer_out = (resid + moe_out).astype(jnp.bfloat16)
    return (layer_out, grad_q.reshape(SEGMENT_WORDS, HD).astype(jnp.bfloat16), grad_k.reshape(SEGMENT_WORDS, HD).astype(jnp.bfloat16), grad_v.reshape(SEGMENT_WORDS, HD).astype(jnp.bfloat16))
```

```python
import functools

import jax
import jax.numpy as jnp
from jax import lax
from jax.experimental import pallas as pl
from jax.experimental.pallas import tpu as pltpu
from jax.sharding import PartitionSpec as P

KERNEL = 4
TOP = 8
EXP_CTX = 2
MESH = pl.DeviceIdType.MESH
BF = jnp.bfloat16
F32 = jnp.float32


def shifted(value, axis, steps):
    count = lax.axis_size(axis)
    first, last = (max(0, -steps), min(count, count - steps))
    return lax.ppermute(value, axis, [(source, source + steps) for source in range(first, last)])


def rms_norm(values, gain):
    return values * lax.rsqrt(jnp.mean(values * values, axis=-1, keepdims=True) + 1e-06) * gain


def greet(axis, n, me, offsets):
    barrier = pltpu.get_barrier_semaphore()
    for r in offsets:
        pl.semaphore_signal(
            barrier, inc=1, device_id={axis: lax.rem(me + r, n)}, device_id_type=MESH
        )
    pl.semaphore_wait(barrier, len(offsets))


def state_kernel(n, rows, give, fwd_out, bwd_out, got, back, land, s1, r1, s2, r2):
    me = lax.axis_index("ctx")
    greet("ctx", n, me, range(1, n))

    def push(source, target, send_sem, recv_sem, r):
        peer = lax.rem(me + r, n)
        return pltpu.make_async_remote_copy(
            src_ref=source.at[peer],
            dst_ref=target.at[me],
            send_sem=send_sem.at[r - 1],
            recv_sem=recv_sem.at[r - 1],
            device_id={"ctx": peer},
            device_id_type=MESH,
        )

    first = [push(give, got, s1, r1, r) for r in range(1, n)]
    for copy in first:
        copy.start()
    got[me] = give[me]
    for copy in first:
        copy.wait()
    state = jnp.zeros((rows, give.shape[2]), F32)
    for k in range(n):
        back[k, 0:rows] = state
        state = got[k, 0:rows] + got[k, 2 * rows : 3 * rows] * state
    state = jnp.zeros((rows, give.shape[2]), F32)
    for k in range(n - 1, -1, -1):
        back[k, rows : 2 * rows] = state
        state = got[k, rows : 2 * rows] + got[k, 2 * rows : 3 * rows] * state
    second = [push(back, land, s2, r2, r) for r in range(1, n)]
    for copy in second:
        copy.start()
    land[me] = back[me]
    for copy in second:
        copy.wait()
    fwd_out[...] = land[:, 0:rows]
    bwd_out[...] = land[:, rows : 2 * rows]


def state_exchange(summary, backsum, block_decay, n):
    heads, size, _ = summary.shape
    rows = heads * size // n
    decay = jnp.broadcast_to(block_decay[:, None, None], (heads, n // heads * rows, size))
    give = jnp.concatenate(
        [
            summary.reshape(n, rows, size),
            backsum.reshape(n, rows, size),
            decay.reshape(n, rows, size),
        ],
        axis=1,
    )
    out = jax.ShapeDtypeStruct((n, rows, size), F32)
    vmem = pl.BlockSpec(memory_space=pltpu.VMEM)
    fwd, bwd = pl.pallas_call(
        functools.partial(state_kernel, n, rows),
        out_shape=(out, out),
        in_specs=[vmem],
        out_specs=(vmem, vmem),
        scratch_shapes=[
            pltpu.VMEM((n, 3 * rows, size), F32),
            pltpu.VMEM((n, 2 * rows, size), F32),
            pltpu.VMEM((n, 2 * rows, size), F32),
        ]
        + [pltpu.SemaphoreType.DMA((n - 1,))] * 4,
        compiler_params=pltpu.CompilerParams(collective_id=1, has_side_effects=True),
        name="state_exchange",
    )(give)
    return fwd.reshape(heads, size, size), bwd.reshape(heads, size, size)


def ring_kernel(n, subs, part, out, right_in, left_in, rs_s, rs_r, ag_s, ag_r):
    me = lax.axis_index("head")
    right, left = lax.rem(me + 1, n), lax.rem(me + n - 1, n)
    greet("head", n, me, (1, n - 1))
    tokens = part.shape[1]
    piece = tokens // (2 * subs)
    ways = ((right, 1, right_in), (left, -1, left_in))

    def span(way, sub):
        return pl.ds((way * subs + sub) * piece, piece)

    def reduce_copy(way, sub, step):
        peer, sign, land = ways[way]
        if step == 0:
            source = part.at[lax.rem(me - sign + n, n), span(way, sub)]
        else:
            source = land.at[step - 1, sub]
        return pltpu.make_async_remote_copy(
            src_ref=source,
            dst_ref=land.at[step, sub],
            send_sem=rs_s.at[way, step, sub],
            recv_sem=rs_r.at[way, step, sub],
            device_id={"head": peer},
            device_id_type=MESH,
        )

    sends = {}
    for sub in range(subs):
        for way in range(2):
            sends[way, sub, 0] = reduce_copy(way, sub, 0)
            sends[way, sub, 0].start()

    def gather_copy(half, sub, way, step):
        peer, sign, _ = ways[way]
        block = lax.rem(me - sign * step + 2 * n, n)
        view = out.at[block, span(half, sub)]
        return pltpu.make_async_remote_copy(
            src_ref=view,
            dst_ref=view,
            send_sem=ag_s.at[half, sub, way, step],
            recv_sem=ag_r.at[half, sub, way, step],
            device_id={"head": peer},
            device_id_type=MESH,
        )

    def hops(half, way):
        return n // 2 if half == way else n // 2 - 1

    gathers = []
    for step in range(n - 1):
        for sub in range(subs):
            for way in range(2):
                _, sign, land = ways[way]
                sends[way, sub, step].wait_recv()
                block = lax.rem(me - sign * (step + 2) + 2 * n, n)
                total = land[step, sub].astype(F32) + part[block, span(way, sub)].astype(F32)
                if step < n - 2:
                    land[step, sub] = total.astype(BF)
                    sends[way, sub, step + 1] = reduce_copy(way, sub, step + 1)
                    sends[way, sub, step + 1].start()
                else:
                    out[me, span(way, sub)] = total.astype(BF)
                    for onward in range(2):
                        copy = gather_copy(way, sub, onward, 0)
                        copy.start()
                        gathers.append(copy)
    for step in range(n // 2):
        for sub in range(subs):
            for half in range(2):
                for way in range(2):
                    if step < hops(half, way):
                        gather_copy(half, sub, way, step).wait_recv()
                        if step + 1 < hops(half, way):
                            copy = gather_copy(half, sub, way, step + 1)
                            copy.start()
                            gathers.append(copy)
    for copy in gathers:
        copy.wait_send()
    for copy in sends.values():
        copy.wait_send()


def ring_sum(part, subs=2):
    n, tokens, cols = part.shape
    piece = tokens // (2 * subs)
    vmem = pl.BlockSpec(memory_space=pltpu.VMEM)
    return pl.pallas_call(
        functools.partial(ring_kernel, n, subs),
        out_shape=jax.ShapeDtypeStruct(part.shape, BF),
        in_specs=[vmem],
        out_specs=vmem,
        scratch_shapes=[
            pltpu.VMEM((n - 1, subs, piece, cols), BF),
            pltpu.VMEM((n - 1, subs, piece, cols), BF),
            pltpu.SemaphoreType.DMA((2, n - 1, subs)),
            pltpu.SemaphoreType.DMA((2, n - 1, subs)),
            pltpu.SemaphoreType.DMA((2, subs, 2, n // 2)),
            pltpu.SemaphoreType.DMA((2, subs, 2, n // 2)),
        ],
        compiler_params=pltpu.CompilerParams(collective_id=2, has_side_effects=True),
        name="ring_sum",
    )(part)


def mm(spec, a, b):
    return jnp.einsum(spec, a.astype(BF), b.astype(BF), preferred_element_type=F32)


def body(
    hidden_in,
    gain_attn,
    w_qkv,
    conv_w,
    log_decay,
    norm_gain,
    w_out,
    gain_moe,
    expert_ids,
    route_weights,
    w_gate,
    w_up,
    w_down,
    grad_core,
):
    n_ctx = lax.axis_size("ctx")
    n_head = lax.axis_size("head")
    my_head = lax.axis_index("head")
    tok_dev, width = hidden_in.shape
    chans = w_qkv.shape[2]
    heads_here = log_decay.shape[1]
    head_size = chans // heads_here
    experts = EXP_CTX * n_ctx
    cap = 3 * tok_dev * TOP // (2 * experts)
    shards = n_head // EXP_CTX
    local_expert = my_head // shards
    cols = width // n_head
    x_float = hidden_in.astype(F32)
    normed = rms_norm(x_float, gain_attn).astype(BF)
    mixed = jnp.einsum("ti,icj->tcj", normed, w_qkv, preferred_element_type=F32).astype(BF)
    rim = shifted(mixed[tok_dev - (KERNEL - 1) :], "ctx", 1)
    padded = jnp.concatenate([rim, mixed], axis=0).astype(F32)
    conv_out = jnp.zeros(mixed.shape, F32)
    for offset in range(KERNEL):
        conv_out = (
            conv_out + conv_w[offset] * padded[KERNEL - 1 - offset : KERNEL - 1 - offset + tok_dev]
        )
    activ = jax.nn.silu(conv_out)
    shape3 = (tok_dev, heads_here, head_size)
    queries = (activ[:, 0] * head_size ** (-0.5)).astype(BF).reshape(shape3)
    keys = activ[:, 1].astype(BF).reshape(shape3)
    vals = activ[:, 2].astype(BF).reshape(shape3)
    cots = grad_core.reshape(shape3)
    steps = jnp.arange(tok_dev)
    cum_decay = jnp.cumsum(log_decay, axis=0)
    cum_t = cum_decay.T
    diff = cum_t[:, :, None] - cum_t[:, None, :]
    lower = (steps[:, None] >= steps[None, :])[None]
    decay_mask = jnp.where(lower, jnp.exp(jnp.where(lower, diff, 0.0)), 0.0)
    tail = jnp.exp(cum_decay[-1][None, :] - cum_decay)[:, :, None]
    lead = jnp.exp(cum_decay)[:, :, None]
    summary = mm("shd,she->hde", keys * tail, vals)
    backsum = mm("thd,the->hde", queries * lead, cots)
    block_decay = jnp.exp(cum_decay[-1])
    state_in, grad_in = state_exchange(summary, backsum, block_decay, n_ctx)
    scores = (mm("thd,shd->hts", queries, keys) * decay_mask).astype(BF)
    attended = mm("hts,shd->thd", scores, vals) + mm("thd,hde->the", queries, state_in) * lead
    headed = rms_norm(attended, norm_gain.reshape(heads_here, head_size)).reshape(tok_dev, chans)
    partial_out = mm("ti,izc->ztc", headed, w_out.reshape(chans, n_head, cols)).astype(BF)
    attn_total = ring_sum(partial_out)

    dov = (mm("thd,shd->hts", cots, vals) * decay_mask).astype(BF)
    grad_q = mm("hts,shd->thd", dov, keys) + lead * mm("the,hde->thd", cots, state_in)
    grad_k = mm("hts,thd->shd", dov, queries) + tail * mm("the,hde->thd", vals, grad_in)
    grad_v = mm("hts,the->she", scores, cots) + tail * mm("thd,hde->the", keys, grad_in)

    resid_full = x_float + attn_total.transpose(1, 0, 2).reshape(tok_dev, width).astype(F32)
    moe_in = rms_norm(resid_full, gain_moe).astype(BF)
    resid_mine = lax.dynamic_slice_in_dim(resid_full, my_head * cols, cols, 1)

    wanted = EXP_CTX * jnp.arange(n_ctx, dtype=jnp.int32)[:, None] + local_expert
    chosen = expert_ids.T[:, None, :] == wanted[None]
    hot = jnp.any(chosen, axis=0)
    earlier = (steps[:, None] < steps[None, :]).astype(BF)
    ranks = mm("et,tu->eu", hot.astype(BF), earlier).astype(jnp.int32)
    slot = jnp.where(hot, ranks, -1)
    weight = jnp.sum(jnp.where(chosen, route_weights.T[:, None, :], 0.0), axis=0)
    taken = slot[:, None, :] == jnp.arange(cap, dtype=jnp.int32)[None, :, None]
    pick = taken.astype(BF)
    share = jnp.where(taken, weight[:, None, :], 0.0).astype(BF)

    buffer = mm("ost,td->osd", pick, moe_in).astype(BF)
    batch = lax.all_to_all(buffer, "ctx", split_axis=0, concat_axis=0, tiled=True)
    gate_val = jnp.einsum("ncd,df->ncf", batch, w_gate[0], preferred_element_type=F32)
    up_val = jnp.einsum("ncd,df->ncf", batch, w_up[0], preferred_element_type=F32)
    inner = (jax.nn.silu(gate_val) * up_val).astype(BF)
    returned = lax.all_to_all(
        jnp.einsum("ncf,fd->ncd", inner, w_down[0], preferred_element_type=F32).astype(BF),
        "ctx",
        split_axis=0,
        concat_axis=0,
        tiled=True,
    )
    total = mm("ost,osd->td", share, returned)
    moe_out = lax.psum_scatter(total.astype(BF), "head", scatter_dimension=1, tiled=True).astype(
        F32
    )
    layer_out = (resid_mine + moe_out).astype(BF)
    return (
        layer_out,
        grad_q.reshape(tok_dev, chans).astype(BF),
        grad_k.reshape(tok_dev, chans).astype(BF),
        grad_v.reshape(tok_dev, chans).astype(BF),
    )


def solution(mesh):
    in_specs = (
        P("ctx", None),
        P(),
        P(None, None, "head"),
        P(None, None, "head"),
        P("ctx", "head"),
        P("head"),
        P("head", None),
        P(),
        P("ctx", None),
        P("ctx", None),
        P(("ctx", "head"), None, None),
        P(("ctx", "head"), None, None),
        P(("ctx", "head"), None, None),
        P("ctx", "head"),
    )
    out_specs = (P("ctx", "head"), P("ctx", "head"), P("ctx", "head"), P("ctx", "head"))
    return jax.shard_map(body, mesh=mesh, in_specs=in_specs, out_specs=out_specs, check_vma=False)
```

```python
import functools

import jax
import jax.numpy as jnp
from jax import lax
from jax.experimental import pallas as pl
from jax.experimental.pallas import tpu as pltpu
from jax.sharding import PartitionSpec as P

KERNEL = 4
TOP = 8
EXP_CTX = 2
MESH = pl.DeviceIdType.MESH
BF = jnp.bfloat16
F32 = jnp.float32


def shifted(value, axis, steps):
    count = lax.axis_size(axis)
    first, last = (max(0, -steps), min(count, count - steps))
    return lax.ppermute(value, axis, [(source, source + steps) for source in range(first, last)])


def rms_norm(values, gain):
    return values * lax.rsqrt(jnp.mean(values * values, axis=-1, keepdims=True) + 1e-06) * gain


def greet(axis, n, me, offsets):
    barrier = pltpu.get_barrier_semaphore()
    for r in offsets:
        pl.semaphore_signal(
            barrier, inc=1, device_id={axis: lax.rem(me + r, n)}, device_id_type=MESH
        )
    pl.semaphore_wait(barrier, len(offsets))


def state_kernel(n, rows, give, fwd_out, bwd_out, got, back, land, s1, r1, s2, r2):
    me = lax.axis_index("ctx")
    greet("ctx", n, me, range(1, n))

    def push(source, target, send_sem, recv_sem, r):
        peer = lax.rem(me + r, n)
        return pltpu.make_async_remote_copy(
            src_ref=source.at[peer],
            dst_ref=target.at[me],
            send_sem=send_sem.at[r - 1],
            recv_sem=recv_sem.at[r - 1],
            device_id={"ctx": peer},
            device_id_type=MESH,
        )

    first = [push(give, got, s1, r1, r) for r in range(1, n)]
    for copy in first:
        copy.start()
    got[me] = give[me]
    for copy in first:
        copy.wait()
    state = jnp.zeros((rows, give.shape[2]), F32)
    for k in range(n):
        back[k, 0:rows] = state
        state = got[k, 0:rows] + got[k, 2 * rows : 3 * rows] * state
    state = jnp.zeros((rows, give.shape[2]), F32)
    for k in range(n - 1, -1, -1):
        back[k, rows : 2 * rows] = state
        state = got[k, rows : 2 * rows] + got[k, 2 * rows : 3 * rows] * state
    second = [push(back, land, s2, r2, r) for r in range(1, n)]
    for copy in second:
        copy.start()
    land[me] = back[me]
    for copy in second:
        copy.wait()
    fwd_out[...] = land[:, 0:rows]
    bwd_out[...] = land[:, rows : 2 * rows]


def state_exchange(summary, backsum, block_decay, n):
    heads, size, _ = summary.shape
    rows = heads * size // n
    decay = jnp.broadcast_to(block_decay[:, None, None], (heads, n // heads * rows, size))
    give = jnp.concatenate(
        [
            summary.reshape(n, rows, size),
            backsum.reshape(n, rows, size),
            decay.reshape(n, rows, size),
        ],
        axis=1,
    )
    out = jax.ShapeDtypeStruct((n, rows, size), F32)
    vmem = pl.BlockSpec(memory_space=pltpu.VMEM)
    fwd, bwd = pl.pallas_call(
        functools.partial(state_kernel, n, rows),
        out_shape=(out, out),
        in_specs=[vmem],
        out_specs=(vmem, vmem),
        scratch_shapes=[
            pltpu.VMEM((n, 3 * rows, size), F32),
            pltpu.VMEM((n, 2 * rows, size), F32),
            pltpu.VMEM((n, 2 * rows, size), F32),
        ]
        + [pltpu.SemaphoreType.DMA((n - 1,))] * 4,
        compiler_params=pltpu.CompilerParams(collective_id=1, has_side_effects=True),
        name="state_exchange",
    )(give)
    return fwd.reshape(heads, size, size), bwd.reshape(heads, size, size)


def hops(n, half, way):
    return n // 2 if half == way else n // 2 - 1


def streams(n, subs):
    return [(half, way, sub) for sub in range(subs) for half in range(2) for way in range(2)]


def ring_reduce(n, subs, part, land, send_sem, recv_sem, finish):
    me = lax.axis_index("head")
    piece = part.shape[1] // (2 * subs)
    signs = (1, -1)

    def block(half, way, step):
        return lax.rem(me + signs[way] * (hops(n, half, way) - step) + n, n)

    def span(half, sub):
        return pl.ds((half * subs + sub) * piece, piece)

    def copy(half, way, sub, step):
        if step == 0:
            source = part.at[block(half, way, 0), span(half, sub)]
        else:
            source = land.at[half, way, sub, step - 1]
        return pltpu.make_async_remote_copy(
            src_ref=source,
            dst_ref=land.at[half, way, sub, step],
            send_sem=send_sem.at[half, way, sub, step],
            recv_sem=recv_sem.at[half, way, sub, step],
            device_id={"head": lax.rem(me + signs[way] + n, n)},
            device_id_type=MESH,
        )

    sent = []

    def go(half, way, sub, step):
        one = copy(half, way, sub, step)
        one.start()
        sent.append(one)

    for stream in streams(n, subs):
        go(*stream, 0)
    for step in range(n // 2):
        for half, way, sub in streams(n, subs):
            last = hops(n, half, way) - 1
            if step > last:
                continue
            copy(half, way, sub, step).wait_recv()
            if step < last:
                own = part[block(half, way, step + 1), span(half, sub)]
                total = land[half, way, sub, step].astype(F32) + own.astype(F32)
                land[half, way, sub, step] = total.astype(BF)
                go(half, way, sub, step + 1)
            elif step == n // 2 - 1:
                other = land[half, 1 - way, sub, hops(n, half, 1 - way) - 1]
                total = land[half, way, sub, step].astype(F32) + other.astype(F32)
                finish(half, sub, span(half, sub), total + part[me, span(half, sub)].astype(F32))
    return sent


def ring_gather(n, subs, out, send_sem, recv_sem):
    me = lax.axis_index("head")
    piece = out.shape[1] // (2 * subs)
    signs = (1, -1)
    sent = []

    def copy(half, way, sub, step):
        owner = lax.rem(me - signs[way] * step + n, n)
        view = out.at[owner, pl.ds((half * subs + sub) * piece, piece)]
        return pltpu.make_async_remote_copy(
            src_ref=view,
            dst_ref=view,
            send_sem=send_sem.at[half, way, sub, step],
            recv_sem=recv_sem.at[half, way, sub, step],
            device_id={"head": lax.rem(me + signs[way] + n, n)},
            device_id_type=MESH,
        )

    def go(half, way, sub, step):
        one = copy(half, way, sub, step)
        one.start()
        sent.append(one)

    def relay():
        for step in range(n // 2):
            for half, way, sub in streams(n, subs):
                if step < hops(n, half, way):
                    arrived = lax.rem(me - signs[way] * (step + 1) + n, n)
                    view = out.at[arrived, pl.ds((half * subs + sub) * piece, piece)]
                    pltpu.make_async_remote_copy(
                        src_ref=view,
                        dst_ref=view,
                        send_sem=send_sem.at[half, way, sub, step],
                        recv_sem=recv_sem.at[half, way, sub, step],
                        device_id={"head": lax.rem(me + signs[way] + n, n)},
                        device_id_type=MESH,
                    ).wait_recv()
                    if step + 1 < hops(n, half, way):
                        go(half, way, sub, step + 1)

    return go, relay, sent


def layer_kernel(
    n,
    n_head,
    cap,
    subs,
    group,
    part,
    x_ref,
    gain_ref,
    slot_ref,
    weight_ref,
    gate_hbm,
    up_hbm,
    down_hbm,
    out_ref,
    attn,
    moe_in,
    pack,
    batch,
    result,
    pair,
    back,
    share,
    gate,
    up,
    down,
    final,
    land,
    land2,
    w_sem,
    rs_s,
    rs_r,
    ag_s,
    ag_r,
    fs_s,
    fs_r,
    go_s,
    go_r,
    zf_s,
    zf_r,
    zr_s,
    zr_r,
    rt_s,
    rt_r,
):
    me = lax.axis_index("ctx")
    me_z = lax.axis_index("head")
    third = cap // 3
    rows = 2 * third
    tokens, width = x_ref.shape
    cols = width // n_head
    odd = lax.rem(me_z, 2)
    partner = me_z + 1 - 2 * odd

    loads = [
        pltpu.make_async_copy(source, target, w_sem.at[i])
        for i, (source, target) in enumerate(((gate_hbm, gate), (up_hbm, up), (down_hbm, down)))
    ]
    for load in loads:
        load.start()

    barrier = pltpu.get_barrier_semaphore()
    for r in range(1, n):
        pl.semaphore_signal(
            barrier, inc=1, device_id={"ctx": lax.rem(me + r, n)}, device_id_type=MESH
        )
    for r in (1, n_head - 1):
        pl.semaphore_signal(
            barrier, inc=1, device_id={"head": lax.rem(me_z + r, n_head)}, device_id_type=MESH
        )
    pl.semaphore_wait(barrier, n + 1)

    start_gather, relay, gathered = ring_gather(n_head, subs, attn, ag_s, ag_r)

    def keep(half, sub, span, total):
        attn[me_z, span] = total.astype(BF)
        for way in range(2):
            start_gather(half, way, sub, 0)

    reduced = ring_reduce(n_head, subs, part, land, rs_s, rs_r, keep)
    relay()

    square = jnp.zeros((tokens, 1), F32)
    for z in range(n_head):
        resid = x_ref[:, z * cols : (z + 1) * cols].astype(F32) + attn[z].astype(F32)
        square = square + jnp.sum(resid * resid, axis=-1, keepdims=True)
    scale = lax.rsqrt(square / width + 1e-06)
    for z in range(n_head):
        view = slice(z * cols, (z + 1) * cols)
        resid = x_ref[:, view].astype(F32) + attn[z].astype(F32)
        moe_in[:, view] = (resid * scale * gain_ref[:, view]).astype(BF)

    row = lax.broadcasted_iota(jnp.int32, (rows, tokens), 0)
    row_slot = jnp.where(row < third, row, row + third * odd)

    def send_copy(r):
        return pltpu.make_async_remote_copy(
            src_ref=pack.at[r],
            dst_ref=batch.at[r, pl.ds(0, rows)],
            send_sem=go_s.at[r],
            recv_sem=go_r.at[r],
            device_id={"ctx": lax.rem(me + r, n)},
            device_id_type=MESH,
        )

    def forward_copy(g):
        some = pl.ds(g * group, group)
        return pltpu.make_async_remote_copy(
            src_ref=batch.at[some, pl.ds(third, third)],
            dst_ref=batch.at[some, pl.ds(rows, third)],
            send_sem=zf_s.at[g],
            recv_sem=zf_r.at[g],
            device_id={"head": partner},
            device_id_type=MESH,
        )

    def pair_copy(g):
        some = pl.ds(g * group, group)
        return pltpu.make_async_remote_copy(
            src_ref=result.at[some, pl.ds(rows, third)],
            dst_ref=pair.at[some],
            send_sem=zr_s.at[g],
            recv_sem=zr_r.at[g],
            device_id={"head": partner},
            device_id_type=MESH,
        )

    def return_copy(r):
        return pltpu.make_async_remote_copy(
            src_ref=result.at[r, pl.ds(0, rows)],
            dst_ref=back.at[r],
            send_sem=rt_s.at[r],
            recv_sem=rt_r.at[r],
            device_id={"ctx": lax.rem(me - r + n, n)},
            device_id_type=MESH,
        )

    def pack_step(step, carry):
        r = lax.rem(step + 1, n)
        dest = lax.rem(me + r, n)
        taken = slot_ref[pl.ds(dest, 1), :] == row_slot
        share[r] = jnp.where(taken, weight_ref[pl.ds(dest, 1), :], 0.0).astype(BF)
        pick = jnp.where(taken, 1.0, 0.0).astype(BF)
        chunk = jnp.dot(pick, moe_in[...], preferred_element_type=F32).astype(BF)

        @pl.when(r > 0)
        def _():
            pack[r] = chunk
            send_copy(r).start()

        @pl.when(r == 0)
        def _():
            batch[0, 0:rows] = chunk

        return carry

    lax.fori_loop(0, n, pack_step, 0)
    for load in loads:
        load.wait()
    groups = n // group

    def expert_step(g, carry):
        @pl.when(g < groups)
        def _():
            for i in range(group):
                r = g * group + i

                @pl.when(r > 0)
                def _():
                    send_copy(r).wait_recv()

            forward_copy(g).start()

        @pl.when(jnp.logical_and(g >= 1, g < groups + 1))
        def _():
            h = g - 1
            forward_copy(h).wait_recv()
            some = pl.ds(h * group, group)
            token = batch[some].reshape(group * cap, width)
            gate_val = jnp.dot(token, gate[...], preferred_element_type=F32)
            up_val = jnp.dot(token, up[...], preferred_element_type=F32)
            inner = (jax.nn.silu(gate_val) * up_val).astype(BF)
            y = jnp.dot(inner, down[...], preferred_element_type=F32).astype(BF)
            result[some] = y.reshape(group, cap, width)
            pair_copy(h).start()

        @pl.when(g >= 2)
        def _():
            h = g - 2
            pair_copy(h).wait_recv()
            some = pl.ds(h * group, group)
            mine = result[some, third:rows].astype(F32) + pair[some].astype(F32)
            result[some, third:rows] = mine.astype(BF)
            for i in range(group):
                r = h * group + i

                @pl.when(r > 0)
                def _():
                    return_copy(r).start()

                @pl.when(r == 0)
                def _():
                    back[0] = result[0, 0:rows]

        return carry

    lax.fori_loop(0, groups + 2, expert_step, 0)

    def arrive(r, carry):
        return_copy(r).wait_recv()
        return carry

    lax.fori_loop(1, n, arrive, 0)
    shares = share[...].reshape(n * rows, tokens)
    for z in range(n_head):
        piece = back[:, :, z * cols : (z + 1) * cols].reshape(n * rows, cols)
        final[z] = lax.dot_general(
            shares, piece, (((0,), (0,)), ((), ())), preferred_element_type=F32
        ).astype(BF)

    mine = pl.ds(pl.multiple_of(me_z * cols, cols), cols)

    def emit(half, sub, span, total):
        resid = x_ref[span, mine].astype(F32) + attn[me_z, span].astype(F32)
        out_ref[span] = (resid + total).astype(BF)

    summed = ring_reduce(n_head, subs, final, land2, fs_s, fs_r, emit)

    for copy in reduced + gathered + summed:
        copy.wait_send()

    def drain(r, carry):
        send_copy(r).wait_send()
        return_copy(r).wait_send()
        return carry

    lax.fori_loop(1, n, drain, 0)

    def drain_pairs(g, carry):
        forward_copy(g).wait_send()
        pair_copy(g).wait_send()
        return carry

    lax.fori_loop(0, groups, drain_pairs, 0)


def layer_tail(part, x, gain, slot, weight, w_gate, w_up, w_down, n, cap, subs=2, group=4):
    n_head, tokens, cols = part.shape
    width = n_head * cols
    rows = 2 * cap // 3
    ffd = w_gate.shape[1]
    piece = tokens // (2 * subs)
    vmem = pl.BlockSpec(memory_space=pltpu.VMEM)
    hbm = pl.BlockSpec(memory_space=pl.ANY)
    dma = pltpu.SemaphoreType.DMA
    ring = dma((2, 2, subs, n_head // 2))
    return pl.pallas_call(
        functools.partial(layer_kernel, n, n_head, cap, subs, group),
        out_shape=jax.ShapeDtypeStruct((tokens, cols), BF),
        in_specs=[vmem] * 5 + [hbm] * 3,
        out_specs=vmem,
        scratch_shapes=[
            pltpu.VMEM((n_head, tokens, cols), BF),
            pltpu.VMEM((tokens, width), BF),
            pltpu.VMEM((n, rows, width), BF),
            pltpu.VMEM((n, cap, width), BF),
            pltpu.VMEM((n, cap, width), BF),
            pltpu.VMEM((n, cap // 3, width), BF),
            pltpu.VMEM((n, rows, width), BF),
            pltpu.VMEM((n, rows, tokens), BF),
            pltpu.VMEM((width, ffd), BF),
            pltpu.VMEM((width, ffd), BF),
            pltpu.VMEM((ffd, width), BF),
            pltpu.VMEM((n_head, tokens, cols), BF),
            pltpu.VMEM((2, 2, subs, n_head // 2, piece, cols), BF),
            pltpu.VMEM((2, 2, subs, n_head // 2, piece, cols), BF),
            dma((3,)),
        ]
        + [ring] * 6
        + [dma((n,))] * 2
        + [dma((n // group,))] * 4
        + [dma((n,))] * 2,
        compiler_params=pltpu.CompilerParams(
            collective_id=2, has_side_effects=True, vmem_limit_bytes=58 << 20
        ),
        name="layer_tail",
    )(part, x, gain.reshape(1, width), slot, weight, w_gate, w_up, w_down)


def mm(spec, a, b):
    return jnp.einsum(spec, a.astype(BF), b.astype(BF), preferred_element_type=F32)


def body(
    hidden_in,
    gain_attn,
    w_qkv,
    conv_w,
    log_decay,
    norm_gain,
    w_out,
    gain_moe,
    expert_ids,
    route_weights,
    w_gate,
    w_up,
    w_down,
    grad_core,
):
    n_ctx = lax.axis_size("ctx")
    n_head = lax.axis_size("head")
    my_head = lax.axis_index("head")
    tok_dev, width = hidden_in.shape
    chans = w_qkv.shape[2]
    heads_here = log_decay.shape[1]
    head_size = chans // heads_here
    experts = EXP_CTX * n_ctx
    cap = 3 * tok_dev * TOP // (2 * experts)
    shards = n_head // EXP_CTX
    local_expert = my_head // shards
    cols = width // n_head
    x_float = hidden_in.astype(F32)
    normed = rms_norm(x_float, gain_attn).astype(BF)
    mixed = jnp.einsum("ti,icj->tcj", normed, w_qkv, preferred_element_type=F32).astype(BF)
    rim = shifted(mixed[tok_dev - (KERNEL - 1) :], "ctx", 1)
    padded = jnp.concatenate([rim, mixed], axis=0).astype(F32)
    conv_out = jnp.zeros(mixed.shape, F32)
    for offset in range(KERNEL):
        conv_out = (
            conv_out + conv_w[offset] * padded[KERNEL - 1 - offset : KERNEL - 1 - offset + tok_dev]
        )
    activ = jax.nn.silu(conv_out)
    shape3 = (tok_dev, heads_here, head_size)
    queries = (activ[:, 0] * head_size ** (-0.5)).astype(BF).reshape(shape3)
    keys = activ[:, 1].astype(BF).reshape(shape3)
    vals = activ[:, 2].astype(BF).reshape(shape3)
    cots = grad_core.reshape(shape3)
    steps = jnp.arange(tok_dev)
    cum_decay = jnp.cumsum(log_decay, axis=0)
    cum_t = cum_decay.T
    diff = cum_t[:, :, None] - cum_t[:, None, :]
    lower = (steps[:, None] >= steps[None, :])[None]
    decay_mask = jnp.where(lower, jnp.exp(jnp.where(lower, diff, 0.0)), 0.0)
    tail = jnp.exp(cum_decay[-1][None, :] - cum_decay)[:, :, None]
    lead = jnp.exp(cum_decay)[:, :, None]
    summary = mm("shd,she->hde", keys * tail, vals)
    backsum = mm("thd,the->hde", queries * lead, cots)
    block_decay = jnp.exp(cum_decay[-1])
    state_in, grad_in = state_exchange(summary, backsum, block_decay, n_ctx)
    scores = (mm("thd,shd->hts", queries, keys) * decay_mask).astype(BF)
    attended = mm("hts,shd->thd", scores, vals) + mm("thd,hde->the", queries, state_in) * lead
    headed = rms_norm(attended, norm_gain.reshape(heads_here, head_size)).reshape(tok_dev, chans)
    partial_out = mm("ti,izc->ztc", headed, w_out.reshape(chans, n_head, cols)).astype(BF)
    dov = (mm("thd,shd->hts", cots, vals) * decay_mask).astype(BF)
    grad_q = mm("hts,shd->thd", dov, keys) + lead * mm("the,hde->thd", cots, state_in)
    grad_k = mm("hts,thd->shd", dov, queries) + tail * mm("the,hde->thd", vals, grad_in)
    grad_v = mm("hts,the->she", scores, cots) + tail * mm("thd,hde->the", keys, grad_in)

    wanted = EXP_CTX * jnp.arange(n_ctx, dtype=jnp.int32)[:, None] + local_expert
    chosen = expert_ids.T[:, None, :] == wanted[None]
    hot = jnp.any(chosen, axis=0)
    earlier = (steps[:, None] < steps[None, :]).astype(BF)
    ranks = mm("et,tu->eu", hot.astype(BF), earlier).astype(jnp.int32)
    slot = jnp.where(hot, ranks, -1)
    weight = jnp.sum(jnp.where(chosen, route_weights.T[:, None, :], 0.0), axis=0)
    layer_out = layer_tail(
        partial_out,
        hidden_in,
        gain_moe,
        slot,
        weight,
        w_gate[0],
        w_up[0],
        w_down[0],
        n_ctx,
        cap,
    )
    return (
        layer_out,
        grad_q.reshape(tok_dev, chans).astype(BF),
        grad_k.reshape(tok_dev, chans).astype(BF),
        grad_v.reshape(tok_dev, chans).astype(BF),
    )


def solution(mesh):
    in_specs = (
        P("ctx", None),
        P(),
        P(None, None, "head"),
        P(None, None, "head"),
        P("ctx", "head"),
        P("head"),
        P("head", None),
        P(),
        P("ctx", None),
        P("ctx", None),
        P(("ctx", "head"), None, None),
        P(("ctx", "head"), None, None),
        P(("ctx", "head"), None, None),
        P("ctx", "head"),
    )
    out_specs = (P("ctx", "head"), P("ctx", "head"), P("ctx", "head"), P("ctx", "head"))
    return jax.shard_map(body, mesh=mesh, in_specs=in_specs, out_specs=out_specs, check_vma=False)
```

```python
import functools

import jax
import jax.numpy as jnp
from jax import lax
from jax.experimental import pallas as pl
from jax.experimental.pallas import tpu as pltpu
from jax.sharding import PartitionSpec as P

KERNEL = 4
TOP = 8
EXP_CTX = 2
MESH = pl.DeviceIdType.MESH
BF = jnp.bfloat16
F32 = jnp.float32


def shifted(value, axis, steps):
    count = lax.axis_size(axis)
    first, last = (max(0, -steps), min(count, count - steps))
    return lax.ppermute(value, axis, [(source, source + steps) for source in range(first, last)])


def rms_norm(values, gain):
    return values * lax.rsqrt(jnp.mean(values * values, axis=-1, keepdims=True) + 1e-06) * gain


def greet(axis, n, me, offsets):
    barrier = pltpu.get_barrier_semaphore()
    for r in offsets:
        pl.semaphore_signal(
            barrier, inc=1, device_id={axis: lax.rem(me + r, n)}, device_id_type=MESH
        )
    pl.semaphore_wait(barrier, len(offsets))


def state_kernel(n, rows, give, fwd_out, bwd_out, got, back, land, s1, r1, s2, r2):
    me = lax.axis_index("ctx")
    greet("ctx", n, me, range(1, n))

    def push(source, target, send_sem, recv_sem, r):
        peer = lax.rem(me + r, n)
        return pltpu.make_async_remote_copy(
            src_ref=source.at[peer],
            dst_ref=target.at[me],
            send_sem=send_sem.at[r - 1],
            recv_sem=recv_sem.at[r - 1],
            device_id={"ctx": peer},
            device_id_type=MESH,
        )

    first = [push(give, got, s1, r1, r) for r in range(1, n)]
    for copy in first:
        copy.start()
    got[me] = give[me]
    for copy in first:
        copy.wait()
    state = jnp.zeros((rows, give.shape[2]), F32)
    for k in range(n):
        back[k, 0:rows] = state
        state = got[k, 0:rows] + got[k, 2 * rows : 3 * rows] * state
    state = jnp.zeros((rows, give.shape[2]), F32)
    for k in range(n - 1, -1, -1):
        back[k, rows : 2 * rows] = state
        state = got[k, rows : 2 * rows] + got[k, 2 * rows : 3 * rows] * state
    second = [push(back, land, s2, r2, r) for r in range(1, n)]
    for copy in second:
        copy.start()
    land[me] = back[me]
    for copy in second:
        copy.wait()
    fwd_out[...] = land[:, 0:rows]
    bwd_out[...] = land[:, rows : 2 * rows]


def state_exchange(summary, backsum, block_decay, n):
    heads, size, _ = summary.shape
    rows = heads * size // n
    decay = jnp.broadcast_to(block_decay[:, None, None], (heads, n // heads * rows, size))
    give = jnp.concatenate(
        [
            summary.reshape(n, rows, size),
            backsum.reshape(n, rows, size),
            decay.reshape(n, rows, size),
        ],
        axis=1,
    )
    out = jax.ShapeDtypeStruct((n, rows, size), F32)
    vmem = pl.BlockSpec(memory_space=pltpu.VMEM)
    fwd, bwd = pl.pallas_call(
        functools.partial(state_kernel, n, rows),
        out_shape=(out, out),
        in_specs=[vmem],
        out_specs=(vmem, vmem),
        scratch_shapes=[
            pltpu.VMEM((n, 3 * rows, size), F32),
            pltpu.VMEM((n, 2 * rows, size), F32),
            pltpu.VMEM((n, 2 * rows, size), F32),
        ]
        + [pltpu.SemaphoreType.DMA((n - 1,))] * 4,
        compiler_params=pltpu.CompilerParams(collective_id=1, has_side_effects=True),
        name="state_exchange",
    )(give)
    return fwd.reshape(heads, size, size), bwd.reshape(heads, size, size)


def hops(n, half, way):
    return n // 2 if half == way else n // 2 - 1


def streams(n, subs):
    return [(half, way, sub) for sub in range(subs) for half in range(2) for way in range(2)]


def ring_reduce(n, subs, part, land, send_sem, recv_sem, finish):
    me = lax.axis_index("head")
    piece = part.shape[1] // (2 * subs)
    signs = (1, -1)

    def block(half, way, step):
        return lax.rem(me + signs[way] * (hops(n, half, way) - step) + n, n)

    def span(half, sub):
        return pl.ds((half * subs + sub) * piece, piece)

    def copy(half, way, sub, step):
        if step == 0:
            source = part.at[block(half, way, 0), span(half, sub)]
        else:
            source = land.at[half, way, sub, step - 1]
        return pltpu.make_async_remote_copy(
            src_ref=source,
            dst_ref=land.at[half, way, sub, step],
            send_sem=send_sem.at[half, way, sub, step],
            recv_sem=recv_sem.at[half, way, sub, step],
            device_id={"head": lax.rem(me + signs[way] + n, n)},
            device_id_type=MESH,
        )

    sent = []

    def go(half, way, sub, step):
        one = copy(half, way, sub, step)
        one.start()
        sent.append(one)

    for stream in streams(n, subs):
        go(*stream, 0)
    for step in range(n // 2):
        for half, way, sub in streams(n, subs):
            last = hops(n, half, way) - 1
            if step > last:
                continue
            copy(half, way, sub, step).wait_recv()
            if step < last:
                own = part[block(half, way, step + 1), span(half, sub)]
                total = land[half, way, sub, step].astype(F32) + own.astype(F32)
                land[half, way, sub, step] = total.astype(BF)
                go(half, way, sub, step + 1)
            elif step == n // 2 - 1:
                other = land[half, 1 - way, sub, hops(n, half, 1 - way) - 1]
                total = land[half, way, sub, step].astype(F32) + other.astype(F32)
                finish(half, sub, span(half, sub), total + part[me, span(half, sub)].astype(F32))
    return sent


def ring_gather(n, subs, out, send_sem, recv_sem):
    me = lax.axis_index("head")
    piece = out.shape[1] // (2 * subs)
    signs = (1, -1)
    sent = []

    def copy(half, way, sub, step):
        owner = lax.rem(me - signs[way] * step + n, n)
        view = out.at[owner, pl.ds((half * subs + sub) * piece, piece)]
        return pltpu.make_async_remote_copy(
            src_ref=view,
            dst_ref=view,
            send_sem=send_sem.at[half, way, sub, step],
            recv_sem=recv_sem.at[half, way, sub, step],
            device_id={"head": lax.rem(me + signs[way] + n, n)},
            device_id_type=MESH,
        )

    def go(half, way, sub, step):
        one = copy(half, way, sub, step)
        one.start()
        sent.append(one)

    def relay():
        for step in range(n // 2):
            for half, way, sub in streams(n, subs):
                if step < hops(n, half, way):
                    arrived = lax.rem(me - signs[way] * (step + 1) + n, n)
                    view = out.at[arrived, pl.ds((half * subs + sub) * piece, piece)]
                    pltpu.make_async_remote_copy(
                        src_ref=view,
                        dst_ref=view,
                        send_sem=send_sem.at[half, way, sub, step],
                        recv_sem=recv_sem.at[half, way, sub, step],
                        device_id={"head": lax.rem(me + signs[way] + n, n)},
                        device_id_type=MESH,
                    ).wait_recv()
                    if step + 1 < hops(n, half, way):
                        go(half, way, sub, step + 1)

    return go, relay, sent


def layer_kernel(
    n,
    n_head,
    cap,
    subs,
    group,
    part,
    x_ref,
    gain_ref,
    slot_ref,
    weight_ref,
    gate_hbm,
    up_hbm,
    down_hbm,
    out_ref,
    attn,
    moe_in,
    pack,
    batch,
    result,
    pair,
    back,
    share,
    gate,
    up,
    down,
    final,
    land,
    land2,
    w_sem,
    rs_s,
    rs_r,
    ag_s,
    ag_r,
    fs_s,
    fs_r,
    go_s,
    go_r,
    zf_s,
    zf_r,
    zr_s,
    zr_r,
    rt_s,
    rt_r,
):
    me = lax.axis_index("ctx")
    me_z = lax.axis_index("head")
    third = cap // 3
    rows = 2 * third
    tokens, width = x_ref.shape
    cols = width // n_head
    odd = lax.rem(me_z, 2)
    partner = me_z + 1 - 2 * odd

    loads = [
        pltpu.make_async_copy(source, target, w_sem.at[i])
        for i, (source, target) in enumerate(((gate_hbm, gate), (up_hbm, up), (down_hbm, down)))
    ]
    for load in loads:
        load.start()

    barrier = pltpu.get_barrier_semaphore()
    for r in range(1, n):
        pl.semaphore_signal(
            barrier, inc=1, device_id={"ctx": lax.rem(me + r, n)}, device_id_type=MESH
        )
    for r in (1, n_head - 1):
        pl.semaphore_signal(
            barrier, inc=1, device_id={"head": lax.rem(me_z + r, n_head)}, device_id_type=MESH
        )
    pl.semaphore_wait(barrier, n + 1)

    start_gather, relay, gathered = ring_gather(n_head, subs, attn, ag_s, ag_r)

    def keep(half, sub, span, total):
        attn[me_z, span] = total.astype(BF)
        for way in range(2):
            start_gather(half, way, sub, 0)

    reduced = ring_reduce(n_head, subs, part, land, rs_s, rs_r, keep)
    relay()

    square = jnp.zeros((tokens, 1), F32)
    for z in range(n_head):
        resid = x_ref[:, z * cols : (z + 1) * cols].astype(F32) + attn[z].astype(F32)
        square = square + jnp.sum(resid * resid, axis=-1, keepdims=True)
    scale = lax.rsqrt(square / width + 1e-06)
    for z in range(n_head):
        view = slice(z * cols, (z + 1) * cols)
        resid = x_ref[:, view].astype(F32) + attn[z].astype(F32)
        moe_in[:, view] = (resid * scale * gain_ref[:, view]).astype(BF)

    row = lax.broadcasted_iota(jnp.int32, (third, tokens), 0)
    row_slots = (row, row + third * (1 + odd))
    groups = n // group

    def distance(g, i):
        return g + i * groups

    def send_copy(part_index, g, i):
        place = g * group + i
        return pltpu.make_async_remote_copy(
            src_ref=pack.at[part_index, place],
            dst_ref=batch.at[part_index, place],
            send_sem=go_s.at[part_index, place],
            recv_sem=go_r.at[part_index, place],
            device_id={"ctx": lax.rem(me + distance(g, i), n)},
            device_id_type=MESH,
        )

    def forward_copy(g):
        some = pl.ds(g * group, group)
        return pltpu.make_async_remote_copy(
            src_ref=batch.at[1, some],
            dst_ref=batch.at[2, some],
            send_sem=zf_s.at[g],
            recv_sem=zf_r.at[g],
            device_id={"head": partner},
            device_id_type=MESH,
        )

    def pair_copy(g):
        some = pl.ds(g * group, group)
        return pltpu.make_async_remote_copy(
            src_ref=result.at[2, some],
            dst_ref=pair.at[some],
            send_sem=zr_s.at[g],
            recv_sem=zr_r.at[g],
            device_id={"head": partner},
            device_id_type=MESH,
        )

    def return_copy(part_index, g, i):
        place = g * group + i
        return pltpu.make_async_remote_copy(
            src_ref=result.at[part_index, place],
            dst_ref=back.at[part_index, place],
            send_sem=rt_s.at[part_index, place],
            recv_sem=rt_r.at[part_index, place],
            device_id={"ctx": lax.rem(me - distance(g, i) + n, n)},
            device_id_type=MESH,
        )

    def each(g, act):
        @pl.when(g > 0)
        def _():
            act(g, 0)

        for i in range(1, group):
            act(g, i)

    for part_index in (1, 0):

        def pack_step(g, carry, part_index=part_index):
            picks = []
            for i in range(group):
                dest = lax.rem(me + distance(g, i), n)
                taken = slot_ref[pl.ds(dest, 1), :] == row_slots[part_index]
                chosen = jnp.where(taken, weight_ref[pl.ds(dest, 1), :], 0.0)
                share[part_index, g * group + i] = chosen.astype(BF)
                picks.append(jnp.where(taken, 1.0, 0.0).astype(BF))
            chunk = jnp.dot(
                jnp.concatenate(picks, axis=0), moe_in[...], preferred_element_type=F32
            ).astype(BF)
            for i in range(group):
                pack[part_index, g * group + i] = chunk[i * third : (i + 1) * third]
            each(g, lambda g, i: send_copy(part_index, g, i).start())

            @pl.when(g == 0)
            def _():
                batch[part_index, 0] = chunk[0:third]

            return carry

        lax.fori_loop(0, groups, pack_step, 0)

    def forward_step(g, carry):
        each(g, lambda g, i: send_copy(1, g, i).wait_recv())
        forward_copy(g).start()
        return carry

    lax.fori_loop(0, groups, forward_step, 0)
    for load in loads:
        load.wait()

    def expert_step(g, carry):
        @pl.when(g < groups)
        def _():
            each(g, lambda g, i: send_copy(0, g, i).wait_recv())
            forward_copy(g).wait_recv()
            some = pl.ds(g * group, group)
            token = batch[:, some].reshape(group * cap, width)
            gate_val = jnp.dot(token, gate[...], preferred_element_type=F32)
            up_val = jnp.dot(token, up[...], preferred_element_type=F32)
            inner = (jax.nn.silu(gate_val) * up_val).astype(BF)
            y = jnp.dot(inner, down[...], preferred_element_type=F32).astype(BF)
            result[:, some] = y.reshape(3, group, third, width)
            pair_copy(g).start()
            each(g, lambda g, i: return_copy(0, g, i).start())

        @pl.when(g == 0)
        def _():
            back[0, 0] = result[0, 0]

        @pl.when(g >= 2)
        def _():
            h = g - 2
            pair_copy(h).wait_recv()
            some = pl.ds(h * group, group)
            mine = result[1, some].astype(F32) + pair[some].astype(F32)
            result[1, some] = mine.astype(BF)
            each(h, lambda h, i: return_copy(1, h, i).start())

        @pl.when(g == 2)
        def _():
            back[1, 0] = result[1, 0]

        return carry

    lax.fori_loop(0, groups + 2, expert_step, 0)

    def arrive(g, carry):
        for part_index in range(2):
            each(g, lambda g, i: return_copy(part_index, g, i).wait_recv())
        return carry

    lax.fori_loop(0, groups, arrive, 0)
    shares = share[...].reshape(n * rows, tokens)
    for z in range(n_head):
        piece = back[:, :, :, z * cols : (z + 1) * cols].reshape(n * rows, cols)
        final[z] = lax.dot_general(
            shares, piece, (((0,), (0,)), ((), ())), preferred_element_type=F32
        ).astype(BF)

    mine = pl.ds(pl.multiple_of(me_z * cols, cols), cols)

    def emit(half, sub, span, total):
        resid = x_ref[span, mine].astype(F32) + attn[me_z, span].astype(F32)
        out_ref[span] = (resid + total).astype(BF)

    summed = ring_reduce(n_head, subs, final, land2, fs_s, fs_r, emit)

    for copy in reduced + gathered + summed:
        copy.wait_send()

    def drain(g, carry):
        for part_index in range(2):
            each(g, lambda g, i: send_copy(part_index, g, i).wait_send())
            each(g, lambda g, i: return_copy(part_index, g, i).wait_send())
        forward_copy(g).wait_send()
        pair_copy(g).wait_send()
        return carry

    lax.fori_loop(0, groups, drain, 0)


def layer_tail(part, x, gain, slot, weight, w_gate, w_up, w_down, n, cap, subs=2, group=4):
    n_head, tokens, cols = part.shape
    width = n_head * cols
    third = cap // 3
    ffd = w_gate.shape[1]
    piece = tokens // (2 * subs)
    vmem = pl.BlockSpec(memory_space=pltpu.VMEM)
    hbm = pl.BlockSpec(memory_space=pl.ANY)
    dma = pltpu.SemaphoreType.DMA
    ring = dma((2, 2, subs, n_head // 2))
    return pl.pallas_call(
        functools.partial(layer_kernel, n, n_head, cap, subs, group),
        out_shape=jax.ShapeDtypeStruct((tokens, cols), BF),
        in_specs=[vmem] * 5 + [hbm] * 3,
        out_specs=vmem,
        scratch_shapes=[
            pltpu.VMEM((n_head, tokens, cols), BF),
            pltpu.VMEM((tokens, width), BF),
            pltpu.VMEM((2, n, third, width), BF),
            pltpu.VMEM((3, n, third, width), BF),
            pltpu.VMEM((3, n, third, width), BF),
            pltpu.VMEM((n, third, width), BF),
            pltpu.VMEM((2, n, third, width), BF),
            pltpu.VMEM((2, n, third, tokens), BF),
            pltpu.VMEM((width, ffd), BF),
            pltpu.VMEM((width, ffd), BF),
            pltpu.VMEM((ffd, width), BF),
            pltpu.VMEM((n_head, tokens, cols), BF),
            pltpu.VMEM((2, 2, subs, n_head // 2, piece, cols), BF),
            pltpu.VMEM((2, 2, subs, n_head // 2, piece, cols), BF),
            dma((3,)),
        ]
        + [ring] * 6
        + [dma((2, n))] * 2
        + [dma((n // group,))] * 4
        + [dma((2, n))] * 2,
        compiler_params=pltpu.CompilerParams(
            collective_id=2, has_side_effects=True, vmem_limit_bytes=58 << 20
        ),
        name="layer_tail",
    )(part, x, gain.reshape(1, width), slot, weight, w_gate, w_up, w_down)


def mm(spec, a, b):
    return jnp.einsum(spec, a.astype(BF), b.astype(BF), preferred_element_type=F32)


def body(
    hidden_in,
    gain_attn,
    w_qkv,
    conv_w,
    log_decay,
    norm_gain,
    w_out,
    gain_moe,
    expert_ids,
    route_weights,
    w_gate,
    w_up,
    w_down,
    grad_core,
):
    n_ctx = lax.axis_size("ctx")
    n_head = lax.axis_size("head")
    my_head = lax.axis_index("head")
    tok_dev, width = hidden_in.shape
    chans = w_qkv.shape[2]
    heads_here = log_decay.shape[1]
    head_size = chans // heads_here
    experts = EXP_CTX * n_ctx
    cap = 3 * tok_dev * TOP // (2 * experts)
    shards = n_head // EXP_CTX
    local_expert = my_head // shards
    cols = width // n_head
    x_float = hidden_in.astype(F32)
    normed = rms_norm(x_float, gain_attn).astype(BF)
    mixed = jnp.einsum("ti,icj->tcj", normed, w_qkv, preferred_element_type=F32).astype(BF)
    rim = shifted(mixed[tok_dev - (KERNEL - 1) :], "ctx", 1)
    padded = jnp.concatenate([rim, mixed], axis=0).astype(F32)
    conv_out = jnp.zeros(mixed.shape, F32)
    for offset in range(KERNEL):
        conv_out = (
            conv_out + conv_w[offset] * padded[KERNEL - 1 - offset : KERNEL - 1 - offset + tok_dev]
        )
    activ = jax.nn.silu(conv_out)
    shape3 = (tok_dev, heads_here, head_size)
    queries = (activ[:, 0] * head_size ** (-0.5)).astype(BF).reshape(shape3)
    keys = activ[:, 1].astype(BF).reshape(shape3)
    vals = activ[:, 2].astype(BF).reshape(shape3)
    cots = grad_core.reshape(shape3)
    steps = jnp.arange(tok_dev)
    cum_decay = jnp.cumsum(log_decay, axis=0)
    cum_t = cum_decay.T
    diff = cum_t[:, :, None] - cum_t[:, None, :]
    lower = (steps[:, None] >= steps[None, :])[None]
    decay_mask = jnp.where(lower, jnp.exp(jnp.where(lower, diff, 0.0)), 0.0)
    tail = jnp.exp(cum_decay[-1][None, :] - cum_decay)[:, :, None]
    lead = jnp.exp(cum_decay)[:, :, None]
    summary = mm("shd,she->hde", keys * tail, vals)
    backsum = mm("thd,the->hde", queries * lead, cots)
    block_decay = jnp.exp(cum_decay[-1])
    state_in, grad_in = state_exchange(summary, backsum, block_decay, n_ctx)
    scores = (mm("thd,shd->hts", queries, keys) * decay_mask).astype(BF)
    attended = mm("hts,shd->thd", scores, vals) + mm("thd,hde->the", queries, state_in) * lead
    headed = rms_norm(attended, norm_gain.reshape(heads_here, head_size)).reshape(tok_dev, chans)
    partial_out = mm("ti,izc->ztc", headed, w_out.reshape(chans, n_head, cols)).astype(BF)
    dov = (mm("thd,shd->hts", cots, vals) * decay_mask).astype(BF)
    grad_q = mm("hts,shd->thd", dov, keys) + lead * mm("the,hde->thd", cots, state_in)
    grad_k = mm("hts,thd->shd", dov, queries) + tail * mm("the,hde->thd", vals, grad_in)
    grad_v = mm("hts,the->she", scores, cots) + tail * mm("thd,hde->the", keys, grad_in)

    wanted = EXP_CTX * jnp.arange(n_ctx, dtype=jnp.int32)[:, None] + local_expert
    chosen = expert_ids.T[:, None, :] == wanted[None]
    hot = jnp.any(chosen, axis=0)
    earlier = (steps[:, None] < steps[None, :]).astype(BF)
    ranks = mm("et,tu->eu", hot.astype(BF), earlier).astype(jnp.int32)
    slot = jnp.where(hot, ranks, -1)
    weight = jnp.sum(jnp.where(chosen, route_weights.T[:, None, :], 0.0), axis=0)
    layer_out = layer_tail(
        partial_out,
        hidden_in,
        gain_moe,
        slot,
        weight,
        w_gate[0],
        w_up[0],
        w_down[0],
        n_ctx,
        cap,
    )
    return (
        layer_out,
        grad_q.reshape(tok_dev, chans).astype(BF),
        grad_k.reshape(tok_dev, chans).astype(BF),
        grad_v.reshape(tok_dev, chans).astype(BF),
    )


def solution(mesh):
    in_specs = (
        P("ctx", None),
        P(),
        P(None, None, "head"),
        P(None, None, "head"),
        P("ctx", "head"),
        P("head"),
        P("head", None),
        P(),
        P("ctx", None),
        P("ctx", None),
        P(("ctx", "head"), None, None),
        P(("ctx", "head"), None, None),
        P(("ctx", "head"), None, None),
        P("ctx", "head"),
    )
    out_specs = (P("ctx", "head"), P("ctx", "head"), P("ctx", "head"), P("ctx", "head"))
    return jax.shard_map(body, mesh=mesh, in_specs=in_specs, out_specs=out_specs, check_vma=False)
```

```python
import functools

import jax
import jax.numpy as jnp
from jax import lax
from jax.experimental import pallas as pl
from jax.experimental.pallas import tpu as pltpu
from jax.sharding import PartitionSpec as P

KERNEL = 4
TOP = 8
EXP_CTX = 2
MESH = pl.DeviceIdType.MESH
BF = jnp.bfloat16
F32 = jnp.float32


def shifted(value, axis, steps):
    count = lax.axis_size(axis)
    first, last = (max(0, -steps), min(count, count - steps))
    return lax.ppermute(value, axis, [(source, source + steps) for source in range(first, last)])


def rms_norm(values, gain):
    return values * lax.rsqrt(jnp.mean(values * values, axis=-1, keepdims=True) + 1e-06) * gain


def greet(axis, n, me, offsets):
    barrier = pltpu.get_barrier_semaphore()
    for r in offsets:
        pl.semaphore_signal(
            barrier, inc=1, device_id={axis: lax.rem(me + r, n)}, device_id_type=MESH
        )
    pl.semaphore_wait(barrier, len(offsets))


def contract(a, b, left, right):
    return lax.dot_general(
        a.astype(BF), b.astype(BF), (((left,), (right,)), ((), ())), preferred_element_type=F32
    )


def core_kernel(
    n,
    heads,
    q,
    k,
    v,
    do,
    cum_col,
    cum_row,
    gain,
    w_out,
    part,
    grad_q,
    grad_k,
    grad_v,
    intra,
    give,
    got,
    back,
    land,
    s1,
    r1,
    s2,
    r2,
):
    me = lax.axis_index("ctx")
    tokens, chans = q.shape
    size = chans // heads
    per = n // heads
    rows = size // per
    greet("ctx", n, me, range(1, n))

    def push(source, target, send_sem, recv_sem, r):
        peer = lax.rem(me + r, n)
        return pltpu.make_async_remote_copy(
            src_ref=source.at[peer],
            dst_ref=target.at[me],
            send_sem=send_sem.at[r - 1],
            recv_sem=recv_sem.at[r - 1],
            device_id={"ctx": peer},
            device_id_type=MESH,
        )

    def view(h):
        return slice(h * size, (h + 1) * size)

    def factors(h):
        cum = cum_col[:, h : h + 1]
        total = cum_row[h : h + 1, tokens - 1 : tokens]
        return jnp.exp(cum), jnp.exp(total - cum), jnp.exp(total)

    for h in range(heads):
        lead, tail, decay = factors(h)
        some = slice(h * per, (h + 1) * per)
        summary = contract(k[:, view(h)].astype(F32) * tail, v[:, view(h)], 0, 0)
        backsum = contract(q[:, view(h)].astype(F32) * lead, do[:, view(h)], 0, 0)
        give[some, 0:rows] = summary.reshape(per, rows, size)
        give[some, rows : 2 * rows] = backsum.reshape(per, rows, size)
        give[some, 2 * rows : 3 * rows] = jnp.broadcast_to(
            decay.reshape(1, 1, 1), (per, rows, size)
        )
    first = [push(give, got, s1, r1, r) for r in range(1, n)]
    for copy in first:
        copy.start()
    got[me] = give[me]

    t_index = lax.broadcasted_iota(jnp.int32, (tokens, tokens), 0)
    s_index = lax.broadcasted_iota(jnp.int32, (tokens, tokens), 1)
    lower = t_index >= s_index
    for h in range(heads):
        qh, kh, vh, dh = q[:, view(h)], k[:, view(h)], v[:, view(h)], do[:, view(h)]
        diff = cum_col[:, h : h + 1] - cum_row[h : h + 1, :]
        mask = jnp.where(lower, jnp.exp(jnp.where(lower, diff, 0.0)), 0.0)
        scores = (contract(qh, kh, 1, 1) * mask).astype(BF)
        dov = (contract(dh, vh, 1, 1) * mask).astype(BF)
        intra[0, :, view(h)] = contract(scores, vh, 1, 0)
        intra[1, :, view(h)] = contract(dov, kh, 1, 0)
        intra[2, :, view(h)] = contract(dov, qh, 0, 0)
        intra[3, :, view(h)] = contract(scores, dh, 0, 0)

    for copy in first:
        copy.wait()
    state = jnp.zeros((rows, size), F32)
    for j in range(n):
        back[j, 0:rows] = state
        state = got[j, 0:rows] + got[j, 2 * rows : 3 * rows] * state
    state = jnp.zeros((rows, size), F32)
    for j in range(n - 1, -1, -1):
        back[j, rows : 2 * rows] = state
        state = got[j, rows : 2 * rows] + got[j, 2 * rows : 3 * rows] * state
    second = [push(back, land, s2, r2, r) for r in range(1, n)]
    for copy in second:
        copy.start()
    land[me] = back[me]
    for copy in second:
        copy.wait()

    headed = []
    for h in range(heads):
        lead, tail, _ = factors(h)
        some = slice(h * per, (h + 1) * per)
        state_in = land[some, 0:rows].reshape(size, size)
        grad_in = land[some, rows : 2 * rows].reshape(size, size)
        attended = intra[0, :, view(h)] + contract(q[:, view(h)], state_in, 1, 0) * lead
        headed.append(rms_norm(attended, gain[:, view(h)]).astype(BF))
        from_state = contract(do[:, view(h)], state_in, 1, 1)
        grad_q[:, view(h)] = (intra[1, :, view(h)] + lead * from_state).astype(BF)
        from_later = contract(v[:, view(h)], grad_in, 1, 1)
        grad_k[:, view(h)] = (intra[2, :, view(h)] + tail * from_later).astype(BF)
        from_later = contract(k[:, view(h)], grad_in, 1, 0)
        grad_v[:, view(h)] = (intra[3, :, view(h)] + tail * from_later).astype(BF)
    headed = jnp.concatenate(headed, axis=1)
    cols = part.shape[2]
    for z in range(part.shape[0]):
        part[z] = contract(headed, w_out[:, z * cols : (z + 1) * cols], 1, 0).astype(BF)


def attention_core(q, k, v, do, cum_decay, gain, w_out, n, n_head):
    tokens, chans = q.shape
    heads = cum_decay.shape[1]
    size = chans // heads
    rows = heads * size // n
    vmem = pl.BlockSpec(memory_space=pltpu.VMEM)
    grad = jax.ShapeDtypeStruct((tokens, chans), BF)
    return pl.pallas_call(
        functools.partial(core_kernel, n, heads),
        out_shape=(
            jax.ShapeDtypeStruct((n_head, tokens, w_out.shape[1] // n_head), BF),
            grad,
            grad,
            grad,
        ),
        in_specs=[vmem] * 8,
        out_specs=(vmem,) * 4,
        scratch_shapes=[
            pltpu.VMEM((4, tokens, chans), F32),
            pltpu.VMEM((n, 3 * rows, size), F32),
            pltpu.VMEM((n, 3 * rows, size), F32),
            pltpu.VMEM((n, 2 * rows, size), F32),
            pltpu.VMEM((n, 2 * rows, size), F32),
        ]
        + [pltpu.SemaphoreType.DMA((n - 1,))] * 4,
        compiler_params=pltpu.CompilerParams(collective_id=1, has_side_effects=True),
        name="attention_core",
    )(q, k, v, do, cum_decay, cum_decay.T, gain.reshape(1, chans), w_out)


def hops(n, half, way):
    return n // 2 if half == way else n // 2 - 1


def streams(n, subs):
    return [(half, way, sub) for sub in range(subs) for half in range(2) for way in range(2)]


def ring_reduce(n, subs, part, land, send_sem, recv_sem, finish):
    me = lax.axis_index("head")
    piece = part.shape[1] // (2 * subs)
    signs = (1, -1)

    def block(half, way, step):
        return lax.rem(me + signs[way] * (hops(n, half, way) - step) + n, n)

    def span(half, sub):
        return pl.ds((half * subs + sub) * piece, piece)

    def copy(half, way, sub, step):
        if step == 0:
            source = part.at[block(half, way, 0), span(half, sub)]
        else:
            source = land.at[half, way, sub, step - 1]
        return pltpu.make_async_remote_copy(
            src_ref=source,
            dst_ref=land.at[half, way, sub, step],
            send_sem=send_sem.at[half, way, sub, step],
            recv_sem=recv_sem.at[half, way, sub, step],
            device_id={"head": lax.rem(me + signs[way] + n, n)},
            device_id_type=MESH,
        )

    sent = []

    def go(half, way, sub, step):
        one = copy(half, way, sub, step)
        one.start()
        sent.append(one)

    for stream in streams(n, subs):
        go(*stream, 0)
    for step in range(n // 2):
        for half, way, sub in streams(n, subs):
            last = hops(n, half, way) - 1
            if step > last:
                continue
            copy(half, way, sub, step).wait_recv()
            if step < last:
                own = part[block(half, way, step + 1), span(half, sub)]
                total = land[half, way, sub, step].astype(F32) + own.astype(F32)
                land[half, way, sub, step] = total.astype(BF)
                go(half, way, sub, step + 1)
            elif step == n // 2 - 1:
                other = land[half, 1 - way, sub, hops(n, half, 1 - way) - 1]
                total = land[half, way, sub, step].astype(F32) + other.astype(F32)
                finish(half, sub, span(half, sub), total + part[me, span(half, sub)].astype(F32))
    return sent


def ring_gather(n, subs, out, send_sem, recv_sem):
    me = lax.axis_index("head")
    piece = out.shape[1] // (2 * subs)
    signs = (1, -1)
    sent = []

    def copy(half, way, sub, step):
        owner = lax.rem(me - signs[way] * step + n, n)
        view = out.at[owner, pl.ds((half * subs + sub) * piece, piece)]
        return pltpu.make_async_remote_copy(
            src_ref=view,
            dst_ref=view,
            send_sem=send_sem.at[half, way, sub, step],
            recv_sem=recv_sem.at[half, way, sub, step],
            device_id={"head": lax.rem(me + signs[way] + n, n)},
            device_id_type=MESH,
        )

    def go(half, way, sub, step):
        one = copy(half, way, sub, step)
        one.start()
        sent.append(one)

    def relay():
        for step in range(n // 2):
            for half, way, sub in streams(n, subs):
                if step < hops(n, half, way):
                    arrived = lax.rem(me - signs[way] * (step + 1) + n, n)
                    view = out.at[arrived, pl.ds((half * subs + sub) * piece, piece)]
                    pltpu.make_async_remote_copy(
                        src_ref=view,
                        dst_ref=view,
                        send_sem=send_sem.at[half, way, sub, step],
                        recv_sem=recv_sem.at[half, way, sub, step],
                        device_id={"head": lax.rem(me + signs[way] + n, n)},
                        device_id_type=MESH,
                    ).wait_recv()
                    if step + 1 < hops(n, half, way):
                        go(half, way, sub, step + 1)

    return go, relay, sent


def layer_kernel(
    n,
    n_head,
    cap,
    subs,
    group,
    part,
    x_ref,
    gain_ref,
    slot_ref,
    weight_ref,
    gate_hbm,
    up_hbm,
    down_hbm,
    out_ref,
    attn,
    moe_in,
    pack,
    batch,
    result,
    pair,
    back,
    share,
    gate,
    up,
    down,
    final,
    land,
    land2,
    w_sem,
    rs_s,
    rs_r,
    ag_s,
    ag_r,
    fs_s,
    fs_r,
    go_s,
    go_r,
    zf_s,
    zf_r,
    zr_s,
    zr_r,
    rt_s,
    rt_r,
):
    me = lax.axis_index("ctx")
    me_z = lax.axis_index("head")
    third = cap // 3
    rows = 2 * third
    tokens, width = x_ref.shape
    cols = width // n_head
    odd = lax.rem(me_z, 2)
    partner = me_z + 1 - 2 * odd

    loads = [
        pltpu.make_async_copy(source, target, w_sem.at[i])
        for i, (source, target) in enumerate(((gate_hbm, gate), (up_hbm, up), (down_hbm, down)))
    ]
    for load in loads:
        load.start()

    barrier = pltpu.get_barrier_semaphore()
    for r in range(1, n):
        pl.semaphore_signal(
            barrier, inc=1, device_id={"ctx": lax.rem(me + r, n)}, device_id_type=MESH
        )
    for r in (1, n_head - 1):
        pl.semaphore_signal(
            barrier, inc=1, device_id={"head": lax.rem(me_z + r, n_head)}, device_id_type=MESH
        )
    pl.semaphore_wait(barrier, n + 1)

    start_gather, relay, gathered = ring_gather(n_head, subs, attn, ag_s, ag_r)

    def keep(half, sub, span, total):
        attn[me_z, span] = total.astype(BF)
        for way in range(2):
            start_gather(half, way, sub, 0)

    reduced = ring_reduce(n_head, subs, part, land, rs_s, rs_r, keep)
    relay()

    square = jnp.zeros((tokens, 1), F32)
    for z in range(n_head):
        resid = x_ref[:, z * cols : (z + 1) * cols].astype(F32) + attn[z].astype(F32)
        square = square + jnp.sum(resid * resid, axis=-1, keepdims=True)
    scale = lax.rsqrt(square / width + 1e-06)
    for z in range(n_head):
        view = slice(z * cols, (z + 1) * cols)
        resid = x_ref[:, view].astype(F32) + attn[z].astype(F32)
        moe_in[:, view] = (resid * scale * gain_ref[:, view]).astype(BF)

    row = lax.broadcasted_iota(jnp.int32, (third, tokens), 0)
    row_slots = (row, row + third * (1 + odd))
    groups = n // group

    def distance(g, i):
        return g + i * groups

    def send_copy(part_index, g, i):
        place = g * group + i
        return pltpu.make_async_remote_copy(
            src_ref=pack.at[part_index, place],
            dst_ref=batch.at[part_index, place],
            send_sem=go_s.at[part_index, place],
            recv_sem=go_r.at[part_index, place],
            device_id={"ctx": lax.rem(me + distance(g, i), n)},
            device_id_type=MESH,
        )

    def forward_copy(g):
        some = pl.ds(g * group, group)
        return pltpu.make_async_remote_copy(
            src_ref=batch.at[1, some],
            dst_ref=batch.at[2, some],
            send_sem=zf_s.at[g],
            recv_sem=zf_r.at[g],
            device_id={"head": partner},
            device_id_type=MESH,
        )

    def pair_copy(g):
        some = pl.ds(g * group, group)
        return pltpu.make_async_remote_copy(
            src_ref=result.at[2, some],
            dst_ref=pair.at[some],
            send_sem=zr_s.at[g],
            recv_sem=zr_r.at[g],
            device_id={"head": partner},
            device_id_type=MESH,
        )

    def return_copy(part_index, g, i):
        place = g * group + i
        return pltpu.make_async_remote_copy(
            src_ref=result.at[part_index, place],
            dst_ref=back.at[part_index, place],
            send_sem=rt_s.at[part_index, place],
            recv_sem=rt_r.at[part_index, place],
            device_id={"ctx": lax.rem(me - distance(g, i) + n, n)},
            device_id_type=MESH,
        )

    def each(g, act):
        @pl.when(g > 0)
        def _():
            act(g, 0)

        for i in range(1, group):
            act(g, i)

    for part_index in (1, 0):

        def pack_step(g, carry, part_index=part_index):
            picks = []
            for i in range(group):
                dest = lax.rem(me + distance(g, i), n)
                taken = slot_ref[pl.ds(dest, 1), :] == row_slots[part_index]
                chosen = jnp.where(taken, weight_ref[pl.ds(dest, 1), :], 0.0)
                share[part_index, g * group + i] = chosen.astype(BF)
                picks.append(jnp.where(taken, 1.0, 0.0).astype(BF))
            chunk = jnp.dot(
                jnp.concatenate(picks, axis=0), moe_in[...], preferred_element_type=F32
            ).astype(BF)
            for i in range(group):
                pack[part_index, g * group + i] = chunk[i * third : (i + 1) * third]
            each(g, lambda g, i: send_copy(part_index, g, i).start())

            @pl.when(g == 0)
            def _():
                batch[part_index, 0] = chunk[0:third]

            return carry

        lax.fori_loop(0, groups, pack_step, 0)

    def forward_step(g, carry):
        each(g, lambda g, i: send_copy(1, g, i).wait_recv())
        forward_copy(g).start()
        return carry

    lax.fori_loop(0, groups, forward_step, 0)
    for load in loads:
        load.wait()

    def expert_step(g, carry):
        @pl.when(g < groups)
        def _():
            each(g, lambda g, i: send_copy(0, g, i).wait_recv())
            forward_copy(g).wait_recv()
            some = pl.ds(g * group, group)
            token = batch[:, some].reshape(group * cap, width)
            gate_val = jnp.dot(token, gate[...], preferred_element_type=F32)
            up_val = jnp.dot(token, up[...], preferred_element_type=F32)
            inner = (jax.nn.silu(gate_val) * up_val).astype(BF)
            y = jnp.dot(inner, down[...], preferred_element_type=F32).astype(BF)
            result[:, some] = y.reshape(3, group, third, width)
            pair_copy(g).start()
            each(g, lambda g, i: return_copy(0, g, i).start())

        @pl.when(g == 0)
        def _():
            back[0, 0] = result[0, 0]

        @pl.when(g >= 2)
        def _():
            h = g - 2
            pair_copy(h).wait_recv()
            some = pl.ds(h * group, group)
            mine = result[1, some].astype(F32) + pair[some].astype(F32)
            result[1, some] = mine.astype(BF)
            each(h, lambda h, i: return_copy(1, h, i).start())

        @pl.when(g == 2)
        def _():
            back[1, 0] = result[1, 0]

        return carry

    lax.fori_loop(0, groups + 2, expert_step, 0)

    def arrive(g, carry):
        for part_index in range(2):
            each(g, lambda g, i: return_copy(part_index, g, i).wait_recv())
        return carry

    lax.fori_loop(0, groups, arrive, 0)
    shares = share[...].reshape(n * rows, tokens)
    for z in range(n_head):
        piece = back[:, :, :, z * cols : (z + 1) * cols].reshape(n * rows, cols)
        final[z] = lax.dot_general(
            shares, piece, (((0,), (0,)), ((), ())), preferred_element_type=F32
        ).astype(BF)

    mine = pl.ds(pl.multiple_of(me_z * cols, cols), cols)

    def emit(half, sub, span, total):
        resid = x_ref[span, mine].astype(F32) + attn[me_z, span].astype(F32)
        out_ref[span] = (resid + total).astype(BF)

    summed = ring_reduce(n_head, subs, final, land2, fs_s, fs_r, emit)

    for copy in reduced + gathered + summed:
        copy.wait_send()

    def drain(g, carry):
        for part_index in range(2):
            each(g, lambda g, i: send_copy(part_index, g, i).wait_send())
            each(g, lambda g, i: return_copy(part_index, g, i).wait_send())
        forward_copy(g).wait_send()
        pair_copy(g).wait_send()
        return carry

    lax.fori_loop(0, groups, drain, 0)


def layer_tail(part, x, gain, slot, weight, w_gate, w_up, w_down, n, cap, subs=2, group=4):
    n_head, tokens, cols = part.shape
    width = n_head * cols
    third = cap // 3
    ffd = w_gate.shape[1]
    piece = tokens // (2 * subs)
    vmem = pl.BlockSpec(memory_space=pltpu.VMEM)
    hbm = pl.BlockSpec(memory_space=pl.ANY)
    dma = pltpu.SemaphoreType.DMA
    ring = dma((2, 2, subs, n_head // 2))
    return pl.pallas_call(
        functools.partial(layer_kernel, n, n_head, cap, subs, group),
        out_shape=jax.ShapeDtypeStruct((tokens, cols), BF),
        in_specs=[vmem] * 5 + [hbm] * 3,
        out_specs=vmem,
        scratch_shapes=[
            pltpu.VMEM((n_head, tokens, cols), BF),
            pltpu.VMEM((tokens, width), BF),
            pltpu.VMEM((2, n, third, width), BF),
            pltpu.VMEM((3, n, third, width), BF),
            pltpu.VMEM((3, n, third, width), BF),
            pltpu.VMEM((n, third, width), BF),
            pltpu.VMEM((2, n, third, width), BF),
            pltpu.VMEM((2, n, third, tokens), BF),
            pltpu.VMEM((width, ffd), BF),
            pltpu.VMEM((width, ffd), BF),
            pltpu.VMEM((ffd, width), BF),
            pltpu.VMEM((n_head, tokens, cols), BF),
            pltpu.VMEM((2, 2, subs, n_head // 2, piece, cols), BF),
            pltpu.VMEM((2, 2, subs, n_head // 2, piece, cols), BF),
            dma((3,)),
        ]
        + [ring] * 6
        + [dma((2, n))] * 2
        + [dma((n // group,))] * 4
        + [dma((2, n))] * 2,
        compiler_params=pltpu.CompilerParams(
            collective_id=2, has_side_effects=True, vmem_limit_bytes=58 << 20
        ),
        name="layer_tail",
    )(part, x, gain.reshape(1, width), slot, weight, w_gate, w_up, w_down)


def mm(spec, a, b):
    return jnp.einsum(spec, a.astype(BF), b.astype(BF), preferred_element_type=F32)


def body(
    hidden_in,
    gain_attn,
    w_qkv,
    conv_w,
    log_decay,
    norm_gain,
    w_out,
    gain_moe,
    expert_ids,
    route_weights,
    w_gate,
    w_up,
    w_down,
    grad_core,
):
    n_ctx = lax.axis_size("ctx")
    n_head = lax.axis_size("head")
    my_head = lax.axis_index("head")
    tok_dev, width = hidden_in.shape
    chans = w_qkv.shape[2]
    heads_here = log_decay.shape[1]
    head_size = chans // heads_here
    experts = EXP_CTX * n_ctx
    cap = 3 * tok_dev * TOP // (2 * experts)
    shards = n_head // EXP_CTX
    local_expert = my_head // shards
    x_float = hidden_in.astype(F32)
    normed = rms_norm(x_float, gain_attn).astype(BF)
    mixed = jnp.einsum("ti,icj->tcj", normed, w_qkv, preferred_element_type=F32).astype(BF)
    rim = shifted(mixed[tok_dev - (KERNEL - 1) :], "ctx", 1)
    padded = jnp.concatenate([rim, mixed], axis=0).astype(F32)
    conv_out = jnp.zeros(mixed.shape, F32)
    for offset in range(KERNEL):
        conv_out = (
            conv_out + conv_w[offset] * padded[KERNEL - 1 - offset : KERNEL - 1 - offset + tok_dev]
        )
    activ = jax.nn.silu(conv_out)
    queries = (activ[:, 0] * head_size ** (-0.5)).astype(BF)
    keys = activ[:, 1].astype(BF)
    vals = activ[:, 2].astype(BF)
    steps = jnp.arange(tok_dev)
    partial_out, grad_q, grad_k, grad_v = attention_core(
        queries,
        keys,
        vals,
        grad_core,
        jnp.cumsum(log_decay, axis=0),
        norm_gain,
        w_out,
        n_ctx,
        n_head,
    )

    wanted = EXP_CTX * jnp.arange(n_ctx, dtype=jnp.int32)[:, None] + local_expert
    chosen = expert_ids.T[:, None, :] == wanted[None]
    hot = jnp.any(chosen, axis=0)
    earlier = (steps[:, None] < steps[None, :]).astype(BF)
    ranks = mm("et,tu->eu", hot.astype(BF), earlier).astype(jnp.int32)
    slot = jnp.where(hot, ranks, -1)
    weight = jnp.sum(jnp.where(chosen, route_weights.T[:, None, :], 0.0), axis=0)
    layer_out = layer_tail(
        partial_out,
        hidden_in,
        gain_moe,
        slot,
        weight,
        w_gate[0],
        w_up[0],
        w_down[0],
        n_ctx,
        cap,
    )
    return (
        layer_out,
        grad_q,
        grad_k,
        grad_v,
    )


def solution(mesh):
    in_specs = (
        P("ctx", None),
        P(),
        P(None, None, "head"),
        P(None, None, "head"),
        P("ctx", "head"),
        P("head"),
        P("head", None),
        P(),
        P("ctx", None),
        P("ctx", None),
        P(("ctx", "head"), None, None),
        P(("ctx", "head"), None, None),
        P(("ctx", "head"), None, None),
        P("ctx", "head"),
    )
    out_specs = (P("ctx", "head"), P("ctx", "head"), P("ctx", "head"), P("ctx", "head"))
    return jax.shard_map(body, mesh=mesh, in_specs=in_specs, out_specs=out_specs, check_vma=False)
```

```python
import functools

import jax
import jax.numpy as jnp
from jax import lax
from jax.experimental import pallas as pl
from jax.experimental.pallas import tpu as pltpu
from jax.sharding import PartitionSpec as P

KERNEL = 4
TOP = 8
EXP_CTX = 2
MESH = pl.DeviceIdType.MESH
BF = jnp.bfloat16
F32 = jnp.float32


def shifted(value, axis, steps):
    count = lax.axis_size(axis)
    first, last = (max(0, -steps), min(count, count - steps))
    return lax.ppermute(value, axis, [(source, source + steps) for source in range(first, last)])


def rms_norm(values, gain):
    return values * lax.rsqrt(jnp.mean(values * values, axis=-1, keepdims=True) + 1e-06) * gain


def greet(axis, n, me, offsets):
    barrier = pltpu.get_barrier_semaphore()
    for r in offsets:
        pl.semaphore_signal(
            barrier, inc=1, device_id={axis: lax.rem(me + r, n)}, device_id_type=MESH
        )
    pl.semaphore_wait(barrier, len(offsets))


def contract(a, b, left, right):
    return lax.dot_general(
        a.astype(BF), b.astype(BF), (((left,), (right,)), ((), ())), preferred_element_type=F32
    )


def core_kernel(
    n,
    heads,
    q,
    k,
    v,
    do,
    log_col,
    log_row,
    gain,
    w_out,
    part,
    grad_q,
    grad_k,
    grad_v,
    intra,
    give,
    got,
    back,
    land,
    s1,
    r1,
    s2,
    r2,
):
    me = lax.axis_index("ctx")
    tokens, chans = q.shape
    size = chans // heads
    per = n // heads
    rows = size // per
    greet("ctx", n, me, range(1, n))

    def push(source, target, send_sem, recv_sem, r):
        peer = lax.rem(me + r, n)
        return pltpu.make_async_remote_copy(
            src_ref=source.at[peer],
            dst_ref=target.at[me],
            send_sem=send_sem.at[r - 1],
            recv_sem=recv_sem.at[r - 1],
            device_id={"ctx": peer},
            device_id_type=MESH,
        )

    t_index = lax.broadcasted_iota(jnp.int32, (tokens, tokens), 0)
    s_index = lax.broadcasted_iota(jnp.int32, (tokens, tokens), 1)
    lower = t_index >= s_index
    cum_col = jnp.dot(
        jnp.where(lower, 1.0, 0.0),
        log_col[...],
        precision=lax.Precision.HIGHEST,
        preferred_element_type=F32,
    )
    cum_row = jnp.dot(
        log_row[...],
        jnp.where(t_index <= s_index, 1.0, 0.0),
        precision=lax.Precision.HIGHEST,
        preferred_element_type=F32,
    )

    def view(h):
        return slice(h * size, (h + 1) * size)

    def factors(h):
        cum = cum_col[:, h : h + 1]
        total = cum_row[h : h + 1, tokens - 1 : tokens]
        return jnp.exp(cum), jnp.exp(total - cum), jnp.exp(total)

    for h in range(heads):
        lead, tail, decay = factors(h)
        some = slice(h * per, (h + 1) * per)
        summary = contract(k[:, view(h)].astype(F32) * tail, v[:, view(h)], 0, 0)
        backsum = contract(q[:, view(h)].astype(F32) * lead, do[:, view(h)], 0, 0)
        give[some, 0:rows] = summary.reshape(per, rows, size)
        give[some, rows : 2 * rows] = backsum.reshape(per, rows, size)
        give[some, 2 * rows : 3 * rows] = jnp.broadcast_to(
            decay.reshape(1, 1, 1), (per, rows, size)
        )
    first = [push(give, got, s1, r1, r) for r in range(1, n)]
    for copy in first:
        copy.start()
    got[me] = give[me]

    for h in range(heads):
        qh, kh, vh, dh = q[:, view(h)], k[:, view(h)], v[:, view(h)], do[:, view(h)]
        diff = cum_col[:, h : h + 1] - cum_row[h : h + 1, :]
        mask = jnp.where(lower, jnp.exp(jnp.where(lower, diff, 0.0)), 0.0)
        scores = (contract(qh, kh, 1, 1) * mask).astype(BF)
        dov = (contract(dh, vh, 1, 1) * mask).astype(BF)
        intra[0, :, view(h)] = contract(scores, vh, 1, 0)
        intra[1, :, view(h)] = contract(dov, kh, 1, 0)
        intra[2, :, view(h)] = contract(dov, qh, 0, 0)
        intra[3, :, view(h)] = contract(scores, dh, 0, 0)

    for copy in first:
        copy.wait()
    state = jnp.zeros((rows, size), F32)
    for j in range(n):
        back[j, 0:rows] = state
        state = got[j, 0:rows] + got[j, 2 * rows : 3 * rows] * state
    state = jnp.zeros((rows, size), F32)
    for j in range(n - 1, -1, -1):
        back[j, rows : 2 * rows] = state
        state = got[j, rows : 2 * rows] + got[j, 2 * rows : 3 * rows] * state
    second = [push(back, land, s2, r2, r) for r in range(1, n)]
    for copy in second:
        copy.start()
    land[me] = back[me]
    for copy in second:
        copy.wait()

    headed = []
    for h in range(heads):
        lead, tail, _ = factors(h)
        some = slice(h * per, (h + 1) * per)
        state_in = land[some, 0:rows].reshape(size, size)
        grad_in = land[some, rows : 2 * rows].reshape(size, size)
        attended = intra[0, :, view(h)] + contract(q[:, view(h)], state_in, 1, 0) * lead
        headed.append(rms_norm(attended, gain[:, view(h)]).astype(BF))
        from_state = contract(do[:, view(h)], state_in, 1, 1)
        grad_q[:, view(h)] = (intra[1, :, view(h)] + lead * from_state).astype(BF)
        from_later = contract(v[:, view(h)], grad_in, 1, 1)
        grad_k[:, view(h)] = (intra[2, :, view(h)] + tail * from_later).astype(BF)
        from_later = contract(k[:, view(h)], grad_in, 1, 0)
        grad_v[:, view(h)] = (intra[3, :, view(h)] + tail * from_later).astype(BF)
    headed = jnp.concatenate(headed, axis=1)
    cols = part.shape[2]
    for z in range(part.shape[0]):
        part[z] = contract(headed, w_out[:, z * cols : (z + 1) * cols], 1, 0).astype(BF)


def attention_core(q, k, v, do, log_decay, gain, w_out, n, n_head):
    tokens, chans = q.shape
    heads = log_decay.shape[1]
    size = chans // heads
    rows = heads * size // n
    vmem = pl.BlockSpec(memory_space=pltpu.VMEM)
    grad = jax.ShapeDtypeStruct((tokens, chans), BF)
    return pl.pallas_call(
        functools.partial(core_kernel, n, heads),
        out_shape=(
            jax.ShapeDtypeStruct((n_head, tokens, w_out.shape[1] // n_head), BF),
            grad,
            grad,
            grad,
        ),
        in_specs=[vmem] * 8,
        out_specs=(vmem,) * 4,
        scratch_shapes=[
            pltpu.VMEM((4, tokens, chans), F32),
            pltpu.VMEM((n, 3 * rows, size), F32),
            pltpu.VMEM((n, 3 * rows, size), F32),
            pltpu.VMEM((n, 2 * rows, size), F32),
            pltpu.VMEM((n, 2 * rows, size), F32),
        ]
        + [pltpu.SemaphoreType.DMA((n - 1,))] * 4,
        compiler_params=pltpu.CompilerParams(collective_id=1, has_side_effects=True),
        name="attention_core",
    )(q, k, v, do, log_decay, log_decay.T, gain.reshape(1, chans), w_out)


def hops(n, half, way):
    return n // 2 if half == way else n // 2 - 1


def streams(n, subs):
    return [(half, way, sub) for sub in range(subs) for half in range(2) for way in range(2)]


def ring_reduce(n, subs, part, land, send_sem, recv_sem, finish):
    me = lax.axis_index("head")
    piece = part.shape[1] // (2 * subs)
    signs = (1, -1)

    def block(half, way, step):
        return lax.rem(me + signs[way] * (hops(n, half, way) - step) + n, n)

    def span(half, sub):
        return pl.ds((half * subs + sub) * piece, piece)

    def copy(half, way, sub, step):
        if step == 0:
            source = part.at[block(half, way, 0), span(half, sub)]
        else:
            source = land.at[half, way, sub, step - 1]
        return pltpu.make_async_remote_copy(
            src_ref=source,
            dst_ref=land.at[half, way, sub, step],
            send_sem=send_sem.at[half, way, sub, step],
            recv_sem=recv_sem.at[half, way, sub, step],
            device_id={"head": lax.rem(me + signs[way] + n, n)},
            device_id_type=MESH,
        )

    sent = []

    def go(half, way, sub, step):
        one = copy(half, way, sub, step)
        one.start()
        sent.append(one)

    for stream in streams(n, subs):
        go(*stream, 0)
    for step in range(n // 2):
        for half, way, sub in streams(n, subs):
            last = hops(n, half, way) - 1
            if step > last:
                continue
            copy(half, way, sub, step).wait_recv()
            if step < last:
                own = part[block(half, way, step + 1), span(half, sub)]
                total = land[half, way, sub, step].astype(F32) + own.astype(F32)
                land[half, way, sub, step] = total.astype(BF)
                go(half, way, sub, step + 1)
            elif step == n // 2 - 1:
                other = land[half, 1 - way, sub, hops(n, half, 1 - way) - 1]
                total = land[half, way, sub, step].astype(F32) + other.astype(F32)
                finish(half, sub, span(half, sub), total + part[me, span(half, sub)].astype(F32))
    return sent


def ring_gather(n, subs, out, send_sem, recv_sem):
    me = lax.axis_index("head")
    piece = out.shape[1] // (2 * subs)
    signs = (1, -1)
    sent = []

    def copy(half, way, sub, step):
        owner = lax.rem(me - signs[way] * step + n, n)
        view = out.at[owner, pl.ds((half * subs + sub) * piece, piece)]
        return pltpu.make_async_remote_copy(
            src_ref=view,
            dst_ref=view,
            send_sem=send_sem.at[half, way, sub, step],
            recv_sem=recv_sem.at[half, way, sub, step],
            device_id={"head": lax.rem(me + signs[way] + n, n)},
            device_id_type=MESH,
        )

    def go(half, way, sub, step):
        one = copy(half, way, sub, step)
        one.start()
        sent.append(one)

    def relay():
        for step in range(n // 2):
            for half, way, sub in streams(n, subs):
                if step < hops(n, half, way):
                    arrived = lax.rem(me - signs[way] * (step + 1) + n, n)
                    view = out.at[arrived, pl.ds((half * subs + sub) * piece, piece)]
                    pltpu.make_async_remote_copy(
                        src_ref=view,
                        dst_ref=view,
                        send_sem=send_sem.at[half, way, sub, step],
                        recv_sem=recv_sem.at[half, way, sub, step],
                        device_id={"head": lax.rem(me + signs[way] + n, n)},
                        device_id_type=MESH,
                    ).wait_recv()
                    if step + 1 < hops(n, half, way):
                        go(half, way, sub, step + 1)

    return go, relay, sent


def layer_kernel(
    n,
    n_head,
    cap,
    subs,
    group,
    part,
    x_ref,
    gain_ref,
    slot_ref,
    weight_ref,
    gate_hbm,
    up_hbm,
    down_hbm,
    out_ref,
    attn,
    moe_in,
    pack,
    batch,
    result,
    pair,
    back,
    share,
    gate,
    up,
    down,
    final,
    land,
    land2,
    w_sem,
    rs_s,
    rs_r,
    ag_s,
    ag_r,
    fs_s,
    fs_r,
    go_s,
    go_r,
    zf_s,
    zf_r,
    zr_s,
    zr_r,
    rt_s,
    rt_r,
):
    me = lax.axis_index("ctx")
    me_z = lax.axis_index("head")
    third = cap // 3
    rows = 2 * third
    tokens, width = x_ref.shape
    cols = width // n_head
    odd = lax.rem(me_z, 2)
    partner = me_z + 1 - 2 * odd

    loads = [
        pltpu.make_async_copy(source, target, w_sem.at[i])
        for i, (source, target) in enumerate(((gate_hbm, gate), (up_hbm, up), (down_hbm, down)))
    ]
    for load in loads:
        load.start()

    barrier = pltpu.get_barrier_semaphore()
    for r in range(1, n):
        pl.semaphore_signal(
            barrier, inc=1, device_id={"ctx": lax.rem(me + r, n)}, device_id_type=MESH
        )
    for r in (1, n_head - 1):
        pl.semaphore_signal(
            barrier, inc=1, device_id={"head": lax.rem(me_z + r, n_head)}, device_id_type=MESH
        )
    pl.semaphore_wait(barrier, n + 1)

    start_gather, relay, gathered = ring_gather(n_head, subs, attn, ag_s, ag_r)

    def keep(half, sub, span, total):
        attn[me_z, span] = total.astype(BF)
        for way in range(2):
            start_gather(half, way, sub, 0)

    reduced = ring_reduce(n_head, subs, part, land, rs_s, rs_r, keep)
    relay()

    square = jnp.zeros((tokens, 1), F32)
    for z in range(n_head):
        resid = x_ref[:, z * cols : (z + 1) * cols].astype(F32) + attn[z].astype(F32)
        square = square + jnp.sum(resid * resid, axis=-1, keepdims=True)
    scale = lax.rsqrt(square / width + 1e-06)
    for z in range(n_head):
        view = slice(z * cols, (z + 1) * cols)
        resid = x_ref[:, view].astype(F32) + attn[z].astype(F32)
        moe_in[:, view] = (resid * scale * gain_ref[:, view]).astype(BF)

    row = lax.broadcasted_iota(jnp.int32, (third, tokens), 0)
    row_slots = (row, row + third * (1 + odd))
    groups = n // group

    def distance(g, i):
        return g + i * groups

    def send_copy(part_index, g, i):
        place = g * group + i
        return pltpu.make_async_remote_copy(
            src_ref=pack.at[part_index, place],
            dst_ref=batch.at[part_index, place],
            send_sem=go_s.at[part_index, place],
            recv_sem=go_r.at[part_index, place],
            device_id={"ctx": lax.rem(me + distance(g, i), n)},
            device_id_type=MESH,
        )

    def forward_copy(g):
        some = pl.ds(g * group, group)
        return pltpu.make_async_remote_copy(
            src_ref=batch.at[1, some],
            dst_ref=batch.at[2, some],
            send_sem=zf_s.at[g],
            recv_sem=zf_r.at[g],
            device_id={"head": partner},
            device_id_type=MESH,
        )

    def pair_copy(g):
        some = pl.ds(g * group, group)
        return pltpu.make_async_remote_copy(
            src_ref=result.at[2, some],
            dst_ref=pair.at[some],
            send_sem=zr_s.at[g],
            recv_sem=zr_r.at[g],
            device_id={"head": partner},
            device_id_type=MESH,
        )

    def return_copy(part_index, g, i):
        place = g * group + i
        return pltpu.make_async_remote_copy(
            src_ref=result.at[part_index, place],
            dst_ref=back.at[part_index, place],
            send_sem=rt_s.at[part_index, place],
            recv_sem=rt_r.at[part_index, place],
            device_id={"ctx": lax.rem(me - distance(g, i) + n, n)},
            device_id_type=MESH,
        )

    def each(g, act):
        @pl.when(g > 0)
        def _():
            act(g, 0)

        for i in range(1, group):
            act(g, i)

    for part_index in (1, 0):

        def pack_step(g, carry, part_index=part_index):
            picks = []
            for i in range(group):
                dest = lax.rem(me + distance(g, i), n)
                taken = slot_ref[pl.ds(dest, 1), :] == row_slots[part_index]
                chosen = jnp.where(taken, weight_ref[pl.ds(dest, 1), :], 0.0)
                share[part_index, g * group + i] = chosen.astype(BF)
                picks.append(jnp.where(taken, 1.0, 0.0).astype(BF))
            chunk = jnp.dot(
                jnp.concatenate(picks, axis=0), moe_in[...], preferred_element_type=F32
            ).astype(BF)
            for i in range(group):
                pack[part_index, g * group + i] = chunk[i * third : (i + 1) * third]
            each(g, lambda g, i: send_copy(part_index, g, i).start())

            @pl.when(g == 0)
            def _():
                batch[part_index, 0] = chunk[0:third]

            return carry

        lax.fori_loop(0, groups, pack_step, 0)

    def forward_step(g, carry):
        each(g, lambda g, i: send_copy(1, g, i).wait_recv())
        forward_copy(g).start()
        return carry

    lax.fori_loop(0, groups, forward_step, 0)
    for load in loads:
        load.wait()

    def expert_step(g, carry):
        @pl.when(g < groups)
        def _():
            each(g, lambda g, i: send_copy(0, g, i).wait_recv())
            forward_copy(g).wait_recv()
            some = pl.ds(g * group, group)
            token = batch[:, some].reshape(group * cap, width)
            gate_val = jnp.dot(token, gate[...], preferred_element_type=F32)
            up_val = jnp.dot(token, up[...], preferred_element_type=F32)
            inner = (jax.nn.silu(gate_val) * up_val).astype(BF)
            y = jnp.dot(inner, down[...], preferred_element_type=F32).astype(BF)
            result[:, some] = y.reshape(3, group, third, width)
            pair_copy(g).start()
            each(g, lambda g, i: return_copy(0, g, i).start())

        @pl.when(g == 0)
        def _():
            back[0, 0] = result[0, 0]

        @pl.when(g >= 2)
        def _():
            h = g - 2
            pair_copy(h).wait_recv()
            some = pl.ds(h * group, group)
            mine = result[1, some].astype(F32) + pair[some].astype(F32)
            result[1, some] = mine.astype(BF)
            each(h, lambda h, i: return_copy(1, h, i).start())

        @pl.when(g == 2)
        def _():
            back[1, 0] = result[1, 0]

        return carry

    lax.fori_loop(0, groups + 2, expert_step, 0)

    def arrive(g, carry):
        for part_index in range(2):
            each(g, lambda g, i: return_copy(part_index, g, i).wait_recv())
        return carry

    lax.fori_loop(0, groups, arrive, 0)
    shares = share[...].reshape(n * rows, tokens)
    for z in range(n_head):
        piece = back[:, :, :, z * cols : (z + 1) * cols].reshape(n * rows, cols)
        final[z] = lax.dot_general(
            shares, piece, (((0,), (0,)), ((), ())), preferred_element_type=F32
        ).astype(BF)

    mine = pl.ds(pl.multiple_of(me_z * cols, cols), cols)

    def emit(half, sub, span, total):
        resid = x_ref[span, mine].astype(F32) + attn[me_z, span].astype(F32)
        out_ref[span] = (resid + total).astype(BF)

    summed = ring_reduce(n_head, subs, final, land2, fs_s, fs_r, emit)

    for copy in reduced + gathered + summed:
        copy.wait_send()

    def drain(g, carry):
        for part_index in range(2):
            each(g, lambda g, i: send_copy(part_index, g, i).wait_send())
            each(g, lambda g, i: return_copy(part_index, g, i).wait_send())
        forward_copy(g).wait_send()
        pair_copy(g).wait_send()
        return carry

    lax.fori_loop(0, groups, drain, 0)


def layer_tail(part, x, gain, slot, weight, w_gate, w_up, w_down, n, cap, subs=2, group=4):
    n_head, tokens, cols = part.shape
    width = n_head * cols
    third = cap // 3
    ffd = w_gate.shape[1]
    piece = tokens // (2 * subs)
    vmem = pl.BlockSpec(memory_space=pltpu.VMEM)
    hbm = pl.BlockSpec(memory_space=pl.ANY)
    dma = pltpu.SemaphoreType.DMA
    ring = dma((2, 2, subs, n_head // 2))
    return pl.pallas_call(
        functools.partial(layer_kernel, n, n_head, cap, subs, group),
        out_shape=jax.ShapeDtypeStruct((tokens, cols), BF),
        in_specs=[vmem] * 5 + [hbm] * 3,
        out_specs=vmem,
        scratch_shapes=[
            pltpu.VMEM((n_head, tokens, cols), BF),
            pltpu.VMEM((tokens, width), BF),
            pltpu.VMEM((2, n, third, width), BF),
            pltpu.VMEM((3, n, third, width), BF),
            pltpu.VMEM((3, n, third, width), BF),
            pltpu.VMEM((n, third, width), BF),
            pltpu.VMEM((2, n, third, width), BF),
            pltpu.VMEM((2, n, third, tokens), BF),
            pltpu.VMEM((width, ffd), BF),
            pltpu.VMEM((width, ffd), BF),
            pltpu.VMEM((ffd, width), BF),
            pltpu.VMEM((n_head, tokens, cols), BF),
            pltpu.VMEM((2, 2, subs, n_head // 2, piece, cols), BF),
            pltpu.VMEM((2, 2, subs, n_head // 2, piece, cols), BF),
            dma((3,)),
        ]
        + [ring] * 6
        + [dma((2, n))] * 2
        + [dma((n // group,))] * 4
        + [dma((2, n))] * 2,
        compiler_params=pltpu.CompilerParams(
            collective_id=2, has_side_effects=True, vmem_limit_bytes=58 << 20
        ),
        name="layer_tail",
    )(part, x, gain.reshape(1, width), slot, weight, w_gate, w_up, w_down)


def mm(spec, a, b):
    return jnp.einsum(spec, a.astype(BF), b.astype(BF), preferred_element_type=F32)


def body(
    hidden_in,
    gain_attn,
    w_qkv,
    conv_w,
    log_decay,
    norm_gain,
    w_out,
    gain_moe,
    expert_ids,
    route_weights,
    w_gate,
    w_up,
    w_down,
    grad_core,
):
    n_ctx = lax.axis_size("ctx")
    n_head = lax.axis_size("head")
    my_head = lax.axis_index("head")
    tok_dev, width = hidden_in.shape
    chans = w_qkv.shape[2]
    heads_here = log_decay.shape[1]
    head_size = chans // heads_here
    experts = EXP_CTX * n_ctx
    cap = 3 * tok_dev * TOP // (2 * experts)
    shards = n_head // EXP_CTX
    local_expert = my_head // shards
    x_float = hidden_in.astype(F32)
    normed = rms_norm(x_float, gain_attn).astype(BF)
    mixed = jnp.einsum("ti,icj->tcj", normed, w_qkv, preferred_element_type=F32).astype(BF)
    rim = shifted(mixed[tok_dev - (KERNEL - 1) :], "ctx", 1)
    padded = jnp.concatenate([rim, mixed], axis=0).astype(F32)
    conv_out = jnp.zeros(mixed.shape, F32)
    for offset in range(KERNEL):
        conv_out = (
            conv_out + conv_w[offset] * padded[KERNEL - 1 - offset : KERNEL - 1 - offset + tok_dev]
        )
    activ = jax.nn.silu(conv_out)
    queries = (activ[:, 0] * head_size ** (-0.5)).astype(BF)
    keys = activ[:, 1].astype(BF)
    vals = activ[:, 2].astype(BF)
    steps = jnp.arange(tok_dev)
    partial_out, grad_q, grad_k, grad_v = attention_core(
        queries,
        keys,
        vals,
        grad_core,
        log_decay,
        norm_gain,
        w_out,
        n_ctx,
        n_head,
    )

    wanted = EXP_CTX * jnp.arange(n_ctx, dtype=jnp.int32)[:, None] + local_expert
    chosen = expert_ids.T[:, None, :] == wanted[None]
    hot = jnp.any(chosen, axis=0)
    earlier = (steps[:, None] < steps[None, :]).astype(BF)
    ranks = mm("et,tu->eu", hot.astype(BF), earlier).astype(jnp.int32)
    slot = jnp.where(hot, ranks, -1)
    weight = jnp.sum(jnp.where(chosen, route_weights.T[:, None, :], 0.0), axis=0)
    layer_out = layer_tail(
        partial_out,
        hidden_in,
        gain_moe,
        slot,
        weight,
        w_gate[0],
        w_up[0],
        w_down[0],
        n_ctx,
        cap,
    )
    return (
        layer_out,
        grad_q,
        grad_k,
        grad_v,
    )


def solution(mesh):
    in_specs = (
        P("ctx", None),
        P(),
        P(None, None, "head"),
        P(None, None, "head"),
        P("ctx", "head"),
        P("head"),
        P("head", None),
        P(),
        P("ctx", None),
        P("ctx", None),
        P(("ctx", "head"), None, None),
        P(("ctx", "head"), None, None),
        P(("ctx", "head"), None, None),
        P("ctx", "head"),
    )
    out_specs = (P("ctx", "head"), P("ctx", "head"), P("ctx", "head"), P("ctx", "head"))
    return jax.shard_map(body, mesh=mesh, in_specs=in_specs, out_specs=out_specs, check_vma=False)
```
